512 devices in a mesh: hist: 16 (over z), rows: 32 (over x, y, core).
Axes of the slice: x: 4, y: 4, z: 16, core: 2. Of those that a mesh axis runs over, the one named last changes fastest.
Arguments:
- g_hist: bfloat16 [352, 64, 352, 128], P('hist', None, 'rows'), may hold values from -0.0390625 to 0.0390625
- g_last: float32 [64, 352, 128], P(None, 'rows'), may hold values from -6 to 6
- integral_last: float32 [64, 352, 128], P(None, 'rows'), may hold values from -6 to 6
- coupling: float32 [64, 64], replicated, may hold values from 0.5 to 2
- step_re: float32 [64, 64], replicated, may hold values from -1 to 2
- step_im: float32 [64, 64], replicated, may hold values from -0.375 to 0.375
Outputs:
- new_row: float32 [64, 352, 128], P('hist', 'rows')
- new_integral: float32 [64, 352, 128], P('hist', 'rows')
The draws below stay inside these ranges and needn't reach their ends.
All inputs are finite; a program needn't handle non-finite values.
Results may differ from the reference program's by a relative error of at most 0.0055.
Values may be sent and summed in bfloat16 or wider, within the bound.
No kernel may reach another device: no remote copies, remote signals or barrier semaphores. Data moves between devices by JAX's collectives and lax.ppermute only.
A program may use at most 64 MiB of HBM per device.

```python
import math
import jax
import jax.numpy as jnp
from jax import lax

NORB = 64
ITERS = 3
NT = 352
H_DEV = 22
N_HIST = 16


def draw_g_last(key, part):
    shape = (NORB, NT, 2 * NORB)
    envelope = (0.5 + jnp.arange(NT, dtype=jnp.float32) / NT)[None, :, None]
    first_key = jax.random.fold_in(jax.random.fold_in(key, 11), 0)
    values = 0.7 * jax.random.normal(first_key, shape, jnp.float32) * envelope
    return jnp.clip(values, -6.0, 6.0)


def draw_step_re(key, part):
    shape = (NORB, NORB)
    first_key = jax.random.fold_in(key, 23)
    noise = jax.random.normal(first_key, shape, jnp.float32)
    values = jnp.eye(NORB, dtype=jnp.float32) + 0.5 * noise / NORB ** 0.5
    return jnp.clip(values, -1.0, 2.0)


def steps_of(own_key, dims, pieces, least, largest):
    def one(position, blocks):
        heights = jax.random.uniform(jax.random.fold_in(jax.random.fold_in(own_key, 6), position), (blocks,), jnp.float32, least / len(pieces), largest / len(pieces))
        return jnp.repeat(jnp.exp(heights), dims[position] // blocks).reshape((-1,) + (1,) * (len(dims) - position - 1))

    loudness = one(*pieces[0])
    for cut in pieces[1:]:
        loudness = loudness * one(*cut)
    return loudness


def bell_draw(own_key, shape, scale, reach, cuts=(), kind=jnp.bfloat16):
    gain = steps_of(own_key, shape, cuts, -0.22, 0.18) if cuts else 1.0
    result = jax.random.normal(own_key, shape, jnp.float32) * scale * gain
    return jnp.minimum(jnp.maximum(result, -reach), reach).astype(kind)


def setup_inputs(seed: int = 0) -> dict:
    streams_of = jax.random.split(jax.random.key(seed), 7)
    return {
        "g_hist": bell_draw(streams_of[0], (NT, NORB, NT, 2 * NORB), (NT * NORB) ** -0.5, 0.0390625, ((0, 16), (2, 32))),
        "g_last": draw_g_last(jax.random.fold_in(streams_of[6], 71), 0),
        "integral_last": bell_draw(streams_of[2], (NORB, NT, 2 * NORB), 1.0, 6.0, ((1, 32),), jnp.float32),
        "coupling": jnp.clip(jnp.exp(jax.random.uniform(streams_of[3], (NORB, NORB), jnp.float32, math.log(0.5), math.log(2.0))), 0.5, 2.0),
        "step_re": draw_step_re(jax.random.fold_in(streams_of[6], 71), 0),
        "step_im": bell_draw(streams_of[5], (NORB, NORB), (4 * NORB) ** -0.5, 0.375, (), jnp.float32),
    }


step_size = 0.5
half_step = 0.25


def combine(first, second, width):
    return jnp.concatenate([first[..., :width] - second[..., width:], first[..., width:] + second[..., :width]], -1)


def apply_step(step_re, step_im, field):
    orbits, times, wide = field.shape
    flat = field.reshape(orbits, times * wide)
    first = jnp.dot(step_re, flat, precision=lax.Precision.HIGHEST, preferred_element_type=jnp.float32).reshape(orbits, times, wide)
    second = jnp.dot(step_im, flat, precision=lax.Precision.HIGHEST, preferred_element_type=jnp.float32).reshape(orbits, times, wide)
    return combine(first, second, orbits)


def density(field):
    orbits = field.shape[0]
    mask = jnp.eye(orbits, dtype=jnp.float32)[:, None, :]
    real_part = field[..., :orbits]
    imag_part = field[..., orbits:]
    return jnp.sum((real_part * real_part + imag_part * imag_part) * mask)


def sigma_of(field, coupling, scale, weights):
    orbits = field.shape[0]
    real_part = field[..., :orbits]
    imag_part = field[..., orbits:]
    factor = coupling[:, None, :] * (real_part * real_part + imag_part * imag_part) / scale * weights[None, :, None]
    return jnp.concatenate([factor * real_part, factor * imag_part], -1).astype(jnp.bfloat16)


def contract(sigma, g_hist):
    real_rows = sigma[..., :NORB].reshape(NORB, NT * NORB)
    imag_rows = sigma[..., NORB:].reshape(NORB, NT * NORB)
    left_side = jnp.concatenate([real_rows, imag_rows], 0)
    lefts = left_side.reshape(2 * NORB, N_HIST, H_DEV * NORB).transpose(1, 0, 2)
    blocks = g_hist.reshape(N_HIST, H_DEV * NORB, NT * 2 * NORB)

    def accumulate(carry, pair):
        return carry + jnp.dot(pair[0].astype(jnp.float32), pair[1].astype(jnp.float32), preferred_element_type=jnp.float32), None

    total, unused = lax.scan(accumulate, jnp.zeros((2 * NORB, NT * 2 * NORB), jnp.float32), (lefts, blocks))
    product = total.reshape(2 * NORB, NT, 2 * NORB)
    return combine(product[:NORB], product[NORB:], NORB)


def reference(g_hist, g_last, integral_last, coupling, step_re, step_im):
    weights = step_size * jnp.where(jnp.arange(NT) == 0, 0.5, 1.0).astype(jnp.float32)
    shifted = jnp.concatenate([g_last[..., :NORB] + half_step * integral_last[..., NORB:], g_last[..., NORB:] - half_step * integral_last[..., :NORB]], -1)
    base = apply_step(step_re, step_im, shifted)
    field = g_last
    integral = integral_last
    for iteration in range(ITERS):
        scale = 1.0 + density(field) / (NT * NORB)
        sigma = sigma_of(field, coupling, scale, weights)
        integral = contract(sigma, g_hist)
        field = base + jnp.concatenate([half_step * integral[..., NORB:], -half_step * integral[..., :NORB]], -1)
    return field, integral
```

```python
import jax
import jax.numpy as jnp
from jax import lax
from jax.sharding import Mesh
from jax.sharding import PartitionSpec as P

ITERS = 3
ROWS = ("rows_0", "rows_1", "rows_2")
EVERY = ("hist", "rows_0", "rows_1", "rows_2")
SMALL = 2.0**-90
LARGE = 2.0**90

step_size = 0.5
half_step = 0.25


def narrow(value):
    return lax.reduce_precision(value, 8, 7)


def rows_of(values, wide):
    return jnp.stack([jnp.broadcast_to(value, (wide,)) for value in values]).astype(jnp.bfloat16)


def halves(value):
    high = narrow(value)
    return high, narrow(value - high)


def on_device(g_hist, g_last, integral_last, coupling, step_re, step_im):
    orbits = g_last.shape[0]
    row_count = g_last.shape[1]
    wide = 2 * orbits
    hist_size = lax.axis_size("hist")
    rows_size = lax.axis_size(ROWS)
    fan_out = rows_size // hist_size
    hist_at = lax.axis_index("hist")
    rows_at = lax.axis_index(ROWS)
    total_cells = row_count * rows_size * orbits
    share = orbits // hist_size
    cells = share * row_count
    padded = -(-(cells + 3) // 16) * 16
    swap = [
        ((z * hist_size + p) * fan_out + k, (p * hist_size + z) * fan_out + k)
        for z in range(hist_size)
        for p in range(hist_size)
        for k in range(fan_out)
    ]

    def my_rows(whole):
        return lax.dynamic_slice_in_dim(whole, hist_at * share, share, 0)

    def fill(rows):
        return jnp.zeros((*rows, padded - cells - 3, wide), jnp.bfloat16)

    part = my_rows(g_last)
    coupling_part = my_rows(coupling)
    moments = rows_at * row_count + jnp.arange(row_count)
    weights = step_size * jnp.where(moments == 0, 0.5, 1.0).astype(jnp.float32)
    factors = coupling_part[:, None, :] * weights[None, :, None]
    mask = (jnp.arange(share)[:, None] + hist_at * share == jnp.arange(orbits)[None, :]).astype(
        jnp.float32
    )

    def piece_of(part, damping):
        real_part = part[..., :orbits]
        imag_part = part[..., orbits:]
        square = real_part * real_part + imag_part * imag_part
        power = jnp.sum(square * mask[:, None, :])
        peak = jnp.max(square)
        factor = factors * (square * damping)
        sigma = jnp.concatenate([factor * real_part, factor * imag_part], -1)
        sigma = sigma.astype(jnp.bfloat16).reshape(cells, wide)
        return jnp.concatenate([sigma, rows_of((*halves(power), peak), wide), fill(())], 0)

    shifted = jnp.concatenate(
        [
            g_last[..., :orbits] + half_step * integral_last[..., orbits:],
            g_last[..., orbits:] - half_step * integral_last[..., :orbits],
        ],
        -1,
    )
    steps = jnp.concatenate([my_rows(step_re), my_rows(step_im)], 0)
    moved = jnp.dot(
        steps,
        shifted.reshape(orbits, row_count * wide),
        precision=lax.Precision.HIGHEST,
        preferred_element_type=jnp.float32,
    ).reshape(2, share, row_count, wide)
    base_part = jnp.concatenate(
        [
            moved[0, ..., :orbits] - moved[1, ..., orbits:],
            moved[0, ..., orbits:] + moved[1, ..., :orbits],
        ],
        -1,
    )
    history = g_hist.reshape(g_hist.shape[0] * orbits, row_count * wide)
    damping, restore = jnp.float32(1.0), jnp.float32(1.0)
    integral_part = part
    for iteration in range(ITERS):
        piece = lax.ppermute(piece_of(part, damping), EVERY, swap)
        copies = jnp.broadcast_to(piece[None], (rows_size, padded, wide))
        pieces = lax.all_to_all(copies, ROWS, split_axis=0, concat_axis=0, tiled=True)
        marks = pieces[:, cells : cells + 3, 0].astype(jnp.float32)
        power = jnp.sum(marks[:, :2])
        peak = jnp.max(marks[:, 2])
        sigma = pieces[:, :cells].reshape(hist_size, fan_out, share, row_count, 2, orbits)
        left = sigma.transpose(4, 0, 2, 1, 3, 5).reshape(wide, fan_out * row_count * orbits)
        product = jnp.dot(left, history, preferred_element_type=jnp.float32)
        product = product.reshape(2, orbits, row_count, wide)
        terms = jnp.concatenate(
            [
                product[0, ..., :orbits] - product[1, ..., orbits:],
                product[0, ..., orbits:] + product[1, ..., :orbits],
            ],
            -1,
        ).astype(jnp.bfloat16)
        terms = terms.reshape(hist_size, cells, wide)
        notes = jnp.broadcast_to(rows_of((*halves(power), peak), wide), (hist_size, 3, wide))
        sent = jnp.concatenate([terms, notes, fill((hist_size,))], 1)
        arrived = lax.all_to_all(sent, "hist", split_axis=0, concat_axis=0, tiled=True)
        marks = arrived[:, cells : cells + 3, 0].astype(jnp.float32)
        scale = 1.0 + jnp.sum(marks[:, :2]) / total_cells
        total = jnp.sum(arrived[:, :cells].astype(jnp.float32), 0)
        integral_part = (total / scale * restore).reshape(share, row_count, wide)
        part = base_part + jnp.concatenate(
            [half_step * integral_part[..., orbits:], -half_step * integral_part[..., :orbits]], -1
        )
        if iteration == 1:
            far = jnp.max(marks[:, 2]) > 2.0**13
            damping = jnp.where(far, SMALL, 1.0)
            restore = jnp.where(far, LARGE, 1.0)
    return (part, integral_part)


def solution(mesh):
    split = Mesh(
        mesh.devices.reshape(mesh.shape["hist"], 4, 4, 2), ("hist", "rows_0", "rows_1", "rows_2")
    )
    return jax.shard_map(
        on_device,
        mesh=split,
        in_specs=(
            P("hist", None, ROWS, None),
            P(None, ROWS, None),
            P(None, ROWS, None),
            P(),
            P(),
            P(),
        ),
        out_specs=(P("hist", ROWS, None), P("hist", ROWS, None)),
        check_vma=False,
    )
```

```python
import functools

import jax
import jax.numpy as jnp
from jax import lax
from jax.experimental import pallas as pl
from jax.experimental.pallas import tpu as pltpu
from jax.sharding import Mesh
from jax.sharding import PartitionSpec as P

ITERS = 3
ROWS = ("rows_0", "rows_1", "rows_2")
EVERY = ("hist", "rows_0", "rows_1", "rows_2")
SMALL = 2.0**-90
LARGE = 2.0**90
FAR = 2.0**13

step_size = 0.5
half_step = 0.25


def low_half(shape):
    return lax.broadcasted_iota(jnp.int32, shape, len(shape) - 1) < shape[-1] // 2


def swapped(value):
    return pltpu.roll(value, value.shape[-1] // 2, axis=value.ndim - 1)


def notes(row, first, power, peak):
    high = power.astype(jnp.bfloat16).astype(jnp.float32)
    parts = (high, power - high, peak)
    value = jnp.zeros(row.shape, jnp.float32)
    for at, part in enumerate(parts):
        value = jnp.where(row == first + at, part, value)
    return value


def write_piece(piece_ref, field, factor_ref, mask_ref, damping, cells):
    row = lax.broadcasted_iota(jnp.int32, field.shape, 0)
    square = field * field
    square = square + swapped(square)
    power = jnp.sum(square * mask_ref[...], axis=(0, 1), keepdims=True)
    peak = jnp.max(jnp.where(row < cells, square, 0.0), axis=(0, 1), keepdims=True)
    sigma = factor_ref[...] * (square * damping) * field
    piece_ref[...] = jnp.where(row < cells, sigma, notes(row, cells, power, peak)).astype(
        piece_ref.dtype
    )


def first_kernel(field_ref, factor_ref, mask_ref, piece_ref, *, cells):
    write_piece(piece_ref, field_ref[...], factor_ref, mask_ref, 1.0, cells)


def advance(arrived_ref, base_ref, restore, cells, total_cells):
    arrived = arrived_ref[...].astype(jnp.float32)
    total = jnp.sum(arrived, axis=0)
    row = lax.broadcasted_iota(jnp.int32, total.shape, 0)
    marked = (row == cells) | (row == cells + 1)
    power = jnp.sum(jnp.where(marked, total, 0.0), axis=0, keepdims=True)
    peak = jnp.max(jnp.where(row == cells + 2, jnp.max(arrived, axis=0), 0.0), axis=0, keepdims=True)
    integral = total / (1.0 + power / total_cells)
    if restore is not None:
        integral = integral * restore
    sign = jnp.where(low_half(total.shape), half_step, -half_step)
    return integral, base_ref[...] + swapped(integral) * sign, peak


def next_kernel(arrived_ref, base_ref, factor_ref, mask_ref, piece_ref, *, cells, total_cells):
    field = advance(arrived_ref, base_ref, None, cells, total_cells)[1]
    write_piece(piece_ref, field, factor_ref, mask_ref, 1.0, cells)


def guarded_kernel(
    arrived_ref, base_ref, factor_ref, mask_ref, piece_ref, restore_ref, *, cells, total_cells
):
    _, field, peak = advance(arrived_ref, base_ref, None, cells, total_cells)
    damping = jnp.where(peak > FAR, SMALL, 1.0)
    restore_ref[...] = jnp.broadcast_to(jnp.where(peak > FAR, LARGE, 1.0), restore_ref.shape)
    write_piece(piece_ref, field, factor_ref, mask_ref, damping, cells)


def last_kernel(arrived_ref, base_ref, restore_ref, row_ref, integral_ref, *, cells, total_cells):
    integral, field, _ = advance(arrived_ref, base_ref, restore_ref[0:1], cells, total_cells)
    row_ref[...] = field[:cells]
    integral_ref[...] = integral[:cells]


def contract_kernel(pieces_ref, history_ref, out_ref, field_ref, left_ref, terms_ref, *, times):
    count, padded, wide = pieces_ref.shape
    groups = padded // 8
    shares = count // 2
    orbits = wide // 2
    upper = lax.broadcasted_iota(jnp.int32, (groups, 8, wide), 1) < 4
    for k in range(2):
        for v in range(shares // 2):
            first = pieces_ref[4 * v + k].astype(jnp.float32).reshape(groups, 8, wide)
            second = pieces_ref[4 * v + 2 + k].astype(jnp.float32).reshape(groups, 8, wide)
            even = jnp.where(upper, first, pltpu.roll(second, 4, axis=1))
            odd = jnp.where(upper, pltpu.roll(first, 4, axis=1), second)
            field_ref[k, 0, :, 8 * v : 8 * v + 8, :] = even
            field_ref[k, 1, :, 8 * v : 8 * v + 8, :] = odd
    low = low_half((orbits, wide))
    for pair in range(times):
        blocks = []
        for s in (2 * pair, 2 * pair + 1):
            k, t = divmod(s, times)
            blocks.append(field_ref[k, t % 2, t // 2])
        lanes = slice(pair * wide, (pair + 1) * wide)
        left_ref[:orbits, lanes] = jnp.where(low, blocks[0], swapped(blocks[1])).astype(jnp.bfloat16)
        left_ref[orbits:, lanes] = jnp.where(low, swapped(blocks[0]), blocks[1]).astype(jnp.bfloat16)
    left = left_ref[...]
    depth = left.shape[1]
    sign = jnp.where(low, -1.0, 1.0)
    which = lax.broadcasted_iota(jnp.int32, (orbits, wide), 0) % 4
    marks = [field_ref[k, 1, groups - 1] for k in range(2)]
    power = jnp.sum(jnp.where(which < 2, marks[0] + marks[1], 0.0), axis=0, keepdims=True)
    peak = jnp.max(
        jnp.where(which == 2, jnp.maximum(marks[0], marks[1]), 0.0), axis=0, keepdims=True
    )
    upper = lax.broadcasted_iota(jnp.int32, (orbits // 8, 8, wide), 1) < 4
    for pair in range(groups):
        moments = [t for t in (2 * pair, 2 * pair + 1) if t < times]
        right = [history_ref[:, t].reshape(depth, wide) for t in moments]
        right = jnp.concatenate(right, -1) if len(right) > 1 else right[0]
        product = jnp.dot(left, right, preferred_element_type=jnp.float32)
        values = []
        for at in range(len(moments)):
            lanes = slice(at * wide, (at + 1) * wide)
            values.append(product[:orbits, lanes] + swapped(product[orbits:, lanes]) * sign)
        if len(moments) < 2:
            values.append(notes(which, 0, power, peak))
        even, odd = (value.reshape(orbits // 8, 8, wide) for value in values)
        terms_ref[:, 0, pair] = jnp.where(upper, even, pltpu.roll(odd, 4, axis=1))
        terms_ref[:, 1, pair] = jnp.where(upper, pltpu.roll(even, 4, axis=1), odd)
    out_ref[...] = terms_ref[...].reshape(shares, padded, wide).astype(out_ref.dtype)


def on_device(g_hist, g_last, integral_last, coupling, step_re, step_im):
    orbits = g_last.shape[0]
    row_count = g_last.shape[1]
    wide = 2 * orbits
    hist_size = lax.axis_size("hist")
    rows_size = lax.axis_size(ROWS)
    fan_out = rows_size // hist_size
    hist_at = lax.axis_index("hist")
    rows_at = lax.axis_index(ROWS)
    total_cells = row_count * rows_size * orbits
    share = orbits // hist_size
    cells = share * row_count
    padded = cells + share
    swap = [
        ((z * hist_size + p) * fan_out + k, (p * hist_size + z) * fan_out + k)
        for z in range(hist_size)
        for p in range(hist_size)
        for k in range(fan_out)
    ]

    def my_rows(whole):
        return lax.dynamic_slice_in_dim(whole, hist_at * share, share, 0)

    def as_rows(value):
        value = value.transpose(1, 0, 2).reshape(cells, wide)
        return jnp.pad(value, ((0, padded - cells), (0, 0)))

    moments = rows_at * row_count + jnp.arange(row_count)
    weights = step_size * jnp.where(moments == 0, 0.5, 1.0).astype(jnp.float32)
    coupling_part = my_rows(coupling)
    twice = jnp.concatenate([coupling_part, coupling_part], -1)
    factor = as_rows(twice[:, None, :] * weights[None, :, None])
    row = jnp.arange(padded)[:, None]
    own = (row % share + hist_at * share == jnp.arange(wide)[None, :]) & (row < cells)
    mask = own.astype(jnp.float32)
    shifted = jnp.concatenate(
        [
            g_last[..., :orbits] + half_step * integral_last[..., orbits:],
            g_last[..., orbits:] - half_step * integral_last[..., :orbits],
        ],
        -1,
    )
    steps = jnp.concatenate([my_rows(step_re), my_rows(step_im)], 0)
    moved = lax.dot_general(
        steps,
        shifted,
        (((1,), (0,)), ((), ())),
        precision=lax.Precision.HIGHEST,
        preferred_element_type=jnp.float32,
    ).reshape(2, share, row_count, wide)
    base = as_rows(
        jnp.concatenate(
            [
                moved[0, ..., :orbits] - moved[1, ..., orbits:],
                moved[0, ..., orbits:] + moved[1, ..., :orbits],
            ],
            -1,
        )
    )
    history = g_hist.transpose(0, 2, 1, 3)
    piece_shape = jax.ShapeDtypeStruct((padded, wide), jnp.bfloat16)
    row_shape = jax.ShapeDtypeStruct((cells, wide), jnp.float32)
    sizes = {"cells": cells, "total_cells": total_cells}
    piece = pl.pallas_call(functools.partial(first_kernel, cells=cells), out_shape=piece_shape)(
        as_rows(my_rows(g_last)), factor, mask
    )
    contract = pl.pallas_call(
        functools.partial(contract_kernel, times=row_count),
        out_shape=jax.ShapeDtypeStruct((hist_size, padded, wide), jnp.bfloat16),
        scratch_shapes=[
            pltpu.VMEM((fan_out, 2, padded // 8, orbits, wide), jnp.float32),
            pltpu.VMEM((wide, fan_out * row_count * orbits), jnp.bfloat16),
            pltpu.VMEM((hist_size // 2, 2, padded // 8, 8, wide), jnp.float32),
        ],
    )
    for iteration in range(ITERS):
        piece = lax.ppermute(piece, EVERY, swap)
        copies = jnp.broadcast_to(piece[None], (rows_size, padded, wide))
        pieces = lax.all_to_all(copies, ROWS, split_axis=0, concat_axis=0, tiled=True)
        sent = contract(pieces, history)
        arrived = lax.all_to_all(sent, "hist", split_axis=0, concat_axis=0, tiled=True)
        if iteration == 0:
            piece = pl.pallas_call(functools.partial(next_kernel, **sizes), out_shape=piece_shape)(
                arrived, base, factor, mask
            )
        elif iteration == 1:
            piece, restore = pl.pallas_call(
                functools.partial(guarded_kernel, **sizes),
                out_shape=(piece_shape, jax.ShapeDtypeStruct((8, wide), jnp.float32)),
            )(arrived, base, factor, mask)
        else:
            new_row, new_integral = pl.pallas_call(
                functools.partial(last_kernel, **sizes), out_shape=(row_shape, row_shape)
            )(arrived, base, restore)

    def as_output(rows):
        return rows.reshape(row_count, share, wide).transpose(1, 0, 2)

    return as_output(new_row), as_output(new_integral)


def solution(mesh):
    split = Mesh(
        mesh.devices.reshape(mesh.shape["hist"], 4, 4, 2), ("hist", "rows_0", "rows_1", "rows_2")
    )
    return jax.shard_map(
        on_device,
        mesh=split,
        in_specs=(
            P("hist", None, ROWS, None),
            P(None, ROWS, None),
            P(None, ROWS, None),
            P(),
            P(),
            P(),
        ),
        out_specs=(P("hist", ROWS, None), P("hist", ROWS, None)),
        check_vma=False,
    )
```

```python
import functools

import jax
import jax.numpy as jnp
from jax import lax
from jax.experimental import pallas as pl
from jax.experimental.pallas import tpu as pltpu
from jax.sharding import Mesh
from jax.sharding import PartitionSpec as P

ITERS = 3
ROWS = ("rows_0", "rows_1", "rows_2")
EVERY = ("hist", "rows_0", "rows_1", "rows_2")
SMALL = 2.0**-90
LARGE = 2.0**90
FAR = 2.0**13

step_size = 0.5
half_step = 0.25


SCALARS = pl.BlockSpec(memory_space=pltpu.SMEM)
VECTORS = pl.BlockSpec(memory_space=pltpu.VMEM)


def call(kernel, shape, specs, scratch=()):
    outs = (VECTORS,) * len(shape) if isinstance(shape, tuple) else VECTORS
    return pl.pallas_call(
        kernel, out_shape=shape, in_specs=specs, out_specs=outs, scratch_shapes=list(scratch)
    )


def places(hist_size):
    side = round(hist_size**0.5)

    def ring(a, b, size):
        return min((a - b) % size, (b - a) % size)

    spots = []
    for p in range(hist_size):
        far_first = sorted(range(hist_size), key=lambda z: (-ring(z, p, hist_size), z))
        near_first = sorted(
            range(hist_size),
            key=lambda q: (ring(q // side, p // side, side) + ring(q % side, p % side, side), q),
        )
        at = dict(zip(far_first, near_first))
        spots.append([at[z] for z in range(hist_size)])
    return spots


def low_half(shape):
    return lax.broadcasted_iota(jnp.int32, shape, len(shape) - 1) < shape[-1] // 2


def swapped(value):
    return pltpu.roll(value, value.shape[-1] // 2, axis=value.ndim - 1)


def notes(row, first, power, peak):
    high = power.astype(jnp.bfloat16).astype(jnp.float32)
    parts = (high, power - high, peak)
    value = jnp.zeros(row.shape, jnp.float32)
    for at, part in enumerate(parts):
        value = jnp.where(row == first + at, part, value)
    return value


def write_piece(piece_ref, field, factor_ref, mask_ref, damping, cells):
    row = lax.broadcasted_iota(jnp.int32, field.shape, 0)
    square = field * field
    square = square + swapped(square)
    power = jnp.sum(square * mask_ref[...], axis=(0, 1), keepdims=True)
    peak = jnp.max(jnp.where(row < cells, square, 0.0), axis=(0, 1), keepdims=True)
    sigma = factor_ref[...] * (square * damping) * field
    piece_ref[...] = jnp.where(row < cells, sigma, notes(row, cells, power, peak)).astype(
        piece_ref.dtype
    )


def first_kernel(
    at_ref, rows_ref, coupling_ref, piece_ref, factor_ref, mask_ref, *, cells, share
):
    hist_at, rows_at = at_ref[0], at_ref[1]
    padded, wide = factor_ref.shape
    groups = padded // 8
    start = pl.multiple_of(hist_at // 2 * 8, 8)
    late = hist_at % 2 == 1
    row = lax.broadcasted_iota(jnp.int32, (8, wide), 0)
    lane = lax.broadcasted_iota(jnp.int32, (8, wide), 1)
    upper = row < share

    def doubled(even, odd):
        up = jnp.where(late, pltpu.roll(even, 4, axis=0), even)
        down = jnp.where(late, odd, pltpu.roll(odd, 4, axis=0))
        return jnp.where(upper, up, down)

    own = coupling_ref[pl.ds(start, 8), :]
    factor = doubled(own, own) * step_size
    mask = jnp.where(lane == hist_at * share + row % share, 1.0, 0.0)
    field = []
    for group in range(groups):
        even = rows_ref[2 * group, pl.ds(start, 8), :]
        last = 2 * group + 1 == rows_ref.shape[0]
        odd = jnp.zeros_like(even) if last else rows_ref[2 * group + 1, pl.ds(start, 8), :]
        field.append(doubled(even, odd))
        scaled = jnp.where(upper & (rows_at == 0), factor * 0.5, factor) if group == 0 else factor
        factor_ref[8 * group : 8 * group + 8, :] = jnp.where(upper, scaled, 0.0) if last else scaled
        mask_ref[8 * group : 8 * group + 8, :] = jnp.where(upper, mask, 0.0) if last else mask
    field = jnp.concatenate(field, 0)
    write_piece(piece_ref, field, factor_ref, mask_ref, 1.0, cells)


def advance(arrived_ref, base_ref, restore, cells, total_cells):
    arrived = arrived_ref[...].astype(jnp.float32)
    total = jnp.sum(arrived, axis=0)
    row = lax.broadcasted_iota(jnp.int32, total.shape, 0)
    marked = (row == cells) | (row == cells + 1)
    power = jnp.sum(jnp.where(marked, total, 0.0), axis=0, keepdims=True)
    peak = jnp.max(jnp.where(row == cells + 2, jnp.max(arrived, axis=0), 0.0), axis=0, keepdims=True)
    integral = total / (1.0 + power / total_cells)
    if restore is not None:
        integral = integral * restore
    sign = jnp.where(low_half(total.shape), half_step, -half_step)
    return integral, base_ref[...] + swapped(integral) * sign, peak


def next_kernel(arrived_ref, base_ref, factor_ref, mask_ref, piece_ref, *, cells, total_cells):
    field = advance(arrived_ref, base_ref, None, cells, total_cells)[1]
    write_piece(piece_ref, field, factor_ref, mask_ref, 1.0, cells)


def guarded_kernel(
    arrived_ref, base_ref, factor_ref, mask_ref, piece_ref, restore_ref, *, cells, total_cells
):
    _, field, peak = advance(arrived_ref, base_ref, None, cells, total_cells)
    damping = jnp.where(peak > FAR, SMALL, 1.0)
    restore_ref[...] = jnp.broadcast_to(jnp.where(peak > FAR, LARGE, 1.0), restore_ref.shape)
    write_piece(piece_ref, field, factor_ref, mask_ref, damping, cells)


def last_kernel(arrived_ref, base_ref, restore_ref, row_ref, integral_ref, *, cells, total_cells):
    integral, field, _ = advance(arrived_ref, base_ref, restore_ref[0:1], cells, total_cells)
    times, share, _ = row_ref.shape
    for t in range(times):
        row_ref[t] = field[t * share : (t + 1) * share]
        integral_ref[t] = integral[t * share : (t + 1) * share]


def contract_kernel(order_ref, pieces_ref, history_ref, out_ref, field_ref, left_ref, terms_ref, *, times):
    count, padded, wide = pieces_ref.shape
    groups = padded // 8
    shares = count // 2
    orbits = wide // 2
    upper = lax.broadcasted_iota(jnp.int32, (groups, 8, wide), 1) < 4
    for k in range(2):
        for v in range(shares // 2):
            first, second = (
                pieces_ref[2 * order_ref[2 * v + at] + k]
                .astype(jnp.float32)
                .reshape(groups, 8, wide)
                for at in range(2)
            )
            even = jnp.where(upper, first, pltpu.roll(second, 4, axis=1))
            odd = jnp.where(upper, pltpu.roll(first, 4, axis=1), second)
            field_ref[k, 0, :, 8 * v : 8 * v + 8, :] = even
            field_ref[k, 1, :, 8 * v : 8 * v + 8, :] = odd
    low = low_half((orbits, wide))
    for pair in range(times):
        blocks = []
        for s in (2 * pair, 2 * pair + 1):
            k, t = divmod(s, times)
            blocks.append(field_ref[k, t % 2, t // 2])
        lanes = slice(pair * wide, (pair + 1) * wide)
        left_ref[:orbits, lanes] = jnp.where(low, blocks[0], swapped(blocks[1])).astype(jnp.bfloat16)
        left_ref[orbits:, lanes] = jnp.where(low, swapped(blocks[0]), blocks[1]).astype(jnp.bfloat16)
    left = left_ref[...]
    depth = left.shape[1]
    sign = jnp.where(low, -1.0, 1.0)
    which = lax.broadcasted_iota(jnp.int32, (orbits, wide), 0) % 4
    marks = [field_ref[k, 1, groups - 1] for k in range(2)]
    power = jnp.sum(jnp.where(which < 2, marks[0] + marks[1], 0.0), axis=0, keepdims=True)
    peak = jnp.max(
        jnp.where(which == 2, jnp.maximum(marks[0], marks[1]), 0.0), axis=0, keepdims=True
    )
    upper = lax.broadcasted_iota(jnp.int32, (orbits // 8, 8, wide), 1) < 4
    for pair in range(groups):
        moments = [t for t in (2 * pair, 2 * pair + 1) if t < times]
        right = [history_ref[:, t].reshape(depth, wide) for t in moments]
        right = jnp.concatenate(right, -1) if len(right) > 1 else right[0]
        product = jnp.dot(left, right, preferred_element_type=jnp.float32)
        values = []
        for at in range(len(moments)):
            lanes = slice(at * wide, (at + 1) * wide)
            values.append(product[:orbits, lanes] + swapped(product[orbits:, lanes]) * sign)
        if len(moments) < 2:
            values.append(notes(which, 0, power, peak))
        even, odd = (value.reshape(orbits // 8, 8, wide) for value in values)
        terms_ref[:, 0, pair] = jnp.where(upper, even, pltpu.roll(odd, 4, axis=1))
        terms_ref[:, 1, pair] = jnp.where(upper, pltpu.roll(even, 4, axis=1), odd)
    out_ref[...] = terms_ref[...].reshape(shares, padded, wide).astype(out_ref.dtype)


def on_device(g_hist, g_last, integral_last, coupling, step_re, step_im):
    orbits = g_last.shape[0]
    row_count = g_last.shape[1]
    wide = 2 * orbits
    hist_size = lax.axis_size("hist")
    rows_size = lax.axis_size(ROWS)
    fan_out = rows_size // hist_size
    hist_at = lax.axis_index("hist")
    rows_at = lax.axis_index(ROWS)
    total_cells = row_count * rows_size * orbits
    share = orbits // hist_size
    cells = share * row_count
    padded = cells + share
    spots = places(hist_size)
    swap = [
        ((z * hist_size + p) * fan_out + k, (p * hist_size + spots[p][z]) * fan_out + k)
        for z in range(hist_size)
        for p in range(hist_size)
        for k in range(fan_out)
    ]
    order = jnp.asarray(spots, jnp.int32)[hist_at]

    def my_rows(whole):
        return lax.dynamic_slice_in_dim(whole, hist_at * share, share, 0)

    def as_rows(value):
        value = value.transpose(1, 0, 2).reshape(cells, wide)
        return jnp.pad(value, ((0, padded - cells), (0, 0)))

    shifted = jnp.concatenate(
        [
            g_last[..., :orbits] + half_step * integral_last[..., orbits:],
            g_last[..., orbits:] - half_step * integral_last[..., :orbits],
        ],
        -1,
    )
    steps = jnp.concatenate([my_rows(step_re), my_rows(step_im)], 0)
    moved = lax.dot_general(
        steps,
        shifted,
        (((1,), (0,)), ((), ())),
        precision=lax.Precision.HIGHEST,
        preferred_element_type=jnp.float32,
    ).reshape(2, share, row_count, wide)
    base = as_rows(
        jnp.concatenate(
            [
                moved[0, ..., :orbits] - moved[1, ..., orbits:],
                moved[0, ..., orbits:] + moved[1, ..., :orbits],
            ],
            -1,
        )
    )
    history = g_hist.transpose(0, 2, 1, 3)
    piece_shape = jax.ShapeDtypeStruct((padded, wide), jnp.bfloat16)
    local_shape = jax.ShapeDtypeStruct((padded, wide), jnp.float32)
    row_shape = jax.ShapeDtypeStruct((row_count, share, wide), jnp.float32)
    sizes = {"cells": cells, "total_cells": total_cells}
    piece, factor, mask = call(
        functools.partial(first_kernel, cells=cells, share=share),
        (piece_shape, local_shape, local_shape),
        (SCALARS, VECTORS, VECTORS),
    )(
        jnp.stack([hist_at, rows_at]).astype(jnp.int32),
        g_last.transpose(1, 0, 2),
        jnp.concatenate([coupling, coupling], -1),
    )
    contract = call(
        functools.partial(contract_kernel, times=row_count),
        jax.ShapeDtypeStruct((hist_size, padded, wide), jnp.bfloat16),
        (SCALARS, VECTORS, VECTORS),
        [
            pltpu.VMEM((fan_out, 2, padded // 8, orbits, wide), jnp.float32),
            pltpu.VMEM((wide, fan_out * row_count * orbits), jnp.bfloat16),
            pltpu.VMEM((hist_size // 2, 2, padded // 8, 8, wide), jnp.float32),
        ],
    )
    for iteration in range(ITERS):
        piece = lax.ppermute(piece, EVERY, swap)
        copies = jnp.broadcast_to(piece[None], (rows_size, padded, wide))
        pieces = lax.all_to_all(copies, ROWS, split_axis=0, concat_axis=0, tiled=True)
        sent = contract(order, pieces, history)
        arrived = lax.all_to_all(sent, "hist", split_axis=0, concat_axis=0, tiled=True)
        if iteration == 0:
            piece = call(functools.partial(next_kernel, **sizes), piece_shape, (VECTORS,) * 4)(
                arrived, base, factor, mask
            )
        elif iteration == 1:
            piece, restore = call(
                functools.partial(guarded_kernel, **sizes),
                (piece_shape, jax.ShapeDtypeStruct((8, wide), jnp.float32)),
                (VECTORS,) * 4,
            )(arrived, base, factor, mask)
        else:
            new_row, new_integral = call(
                functools.partial(last_kernel, **sizes), (row_shape, row_shape), (VECTORS,) * 3
            )(arrived, base, restore)
    return new_row.transpose(1, 0, 2), new_integral.transpose(1, 0, 2)


def solution(mesh):
    split = Mesh(
        mesh.devices.reshape(mesh.shape["hist"], 4, 4, 2), ("hist", "rows_0", "rows_1", "rows_2")
    )
    return jax.shard_map(
        on_device,
        mesh=split,
        in_specs=(
            P("hist", None, ROWS, None),
            P(None, ROWS, None),
            P(None, ROWS, None),
            P(),
            P(),
            P(),
        ),
        out_specs=(P("hist", ROWS, None), P("hist", ROWS, None)),
        check_vma=False,
    )
```

```python
import functools

import jax
import jax.numpy as jnp
from jax import lax
from jax.experimental import pallas as pl
from jax.experimental.pallas import tpu as pltpu
from jax.sharding import Mesh
from jax.sharding import PartitionSpec as P

ITERS = 3
PLANE = ("rows_0", "rows_1")
ROWS = (*PLANE, "rows_2")
SMALL = 2.0**-90
LARGE = 2.0**90
FAR = 2.0**13

step_size = 0.5
half_step = 0.25


def halves(value):
    high = lax.reduce_precision(value, 8, 7)
    return high, lax.reduce_precision(value - high, 8, 7)


SCALARS = pl.BlockSpec(memory_space=pltpu.SMEM)
VECTORS = pl.BlockSpec(memory_space=pltpu.VMEM)


def call(kernel, shape, specs, scratch=()):
    outs = (VECTORS,) * len(shape) if isinstance(shape, tuple) else VECTORS
    return pl.pallas_call(
        kernel,
        out_shape=shape,
        in_specs=specs,
        out_specs=outs,
        scratch_shapes=list(scratch),
        compiler_params=pltpu.CompilerParams(vmem_limit_bytes=16 * 2**20),
    )


def low_half(shape):
    return lax.broadcasted_iota(jnp.int32, shape, len(shape) - 1) < shape[-1] // 2


def swapped(value):
    return pltpu.roll(value, value.shape[-1] // 2, axis=value.ndim - 1)


def notes(row, first, power, peak):
    high = power.astype(jnp.bfloat16).astype(jnp.float32)
    parts = (high, power - high, peak)
    value = jnp.zeros(row.shape, jnp.float32)
    for at, part in enumerate(parts):
        value = jnp.where(row == first + at, part, value)
    return value


def write_piece(piece_ref, field, factor_ref, mask_ref, damping, cells):
    row = lax.broadcasted_iota(jnp.int32, field.shape, 0)
    square = field * field
    square = square + swapped(square)
    power = jnp.sum(square * mask_ref[...], axis=(0, 1), keepdims=True)
    peak = jnp.max(jnp.where(row < cells, square, 0.0), axis=(0, 1), keepdims=True)
    sigma = factor_ref[...] * (square * damping) * field
    piece_ref[...] = jnp.where(row < cells, sigma, notes(row, cells, power, peak)).astype(
        piece_ref.dtype
    )


def packed(even, odd):
    even, odd = (value.reshape(-1, 8, value.shape[-1]) for value in (even, odd))
    upper = lax.broadcasted_iota(jnp.int32, even.shape, 1) < 4
    return (
        jnp.where(upper, even, pltpu.roll(odd, 4, axis=1)),
        jnp.where(upper, pltpu.roll(even, 4, axis=1), odd),
    )


def first_kernel(
    at_ref, rows_ref, coupling_ref, pieces_ref, factor_ref, mask_ref, terms_ref, *, share
):
    rows_at, plane_at, block_at = at_ref[0], at_ref[1], at_ref[2]
    times, orbits, wide = rows_ref.shape
    count, padded, _ = pieces_ref.shape
    row = lax.broadcasted_iota(jnp.int32, (orbits, wide), 0)
    lane = lax.broadcasted_iota(jnp.int32, (orbits, wide), 1)
    own = coupling_ref[...] * step_size
    power = jnp.zeros((orbits, wide), jnp.float32)
    peak = jnp.zeros((orbits, wide), jnp.float32)
    values = []
    for t in range(times):
        field = rows_ref[t]
        square = field * field
        square = square + swapped(square)
        power = power + jnp.where(lane == row, square, 0.0)
        peak = jnp.maximum(peak, square)
        scaled = jnp.where(rows_at == 0, own * 0.5, own) if t == 0 else own
        values.append(scaled * square * field)
    power = jnp.sum(power, axis=(0, 1), keepdims=True)
    peak = jnp.max(peak, axis=(0, 1), keepdims=True)
    values.append(notes(row % share, 0, jnp.where(row < share, power, 0.0), peak))
    for pair in range(padded // 8):
        terms_ref[:, 0, pair], terms_ref[:, 1, pair] = packed(*values[2 * pair : 2 * pair + 2])
    pieces_ref[...] = terms_ref[...].reshape(count, padded, wide).astype(pieces_ref.dtype)

    start = pl.multiple_of(plane_at // 2 * 8, 8)
    mine = coupling_ref[pl.ds(start, 8), :] * step_size
    turned = pltpu.roll(mine, 4, axis=0)
    row = lax.broadcasted_iota(jnp.int32, mine.shape, 0)
    lane = lax.broadcasted_iota(jnp.int32, mine.shape, 1)
    upper = row < share
    factor = jnp.where(upper == (plane_at % 2 == 0), mine, turned)
    mask = jnp.where(lane == plane_at * share + row % share, 1.0, 0.0)
    for group in range(padded // 8):
        scaled, kept = factor, mask
        if group == 0:
            scaled = jnp.where(upper & (block_at == 0), factor * 0.5, factor)
        if 2 * group + 1 == times:
            scaled, kept = jnp.where(upper, factor, 0.0), jnp.where(upper, mask, 0.0)
        factor_ref[8 * group : 8 * group + 8, :] = scaled
        mask_ref[8 * group : 8 * group + 8, :] = kept


def advance(arrived_ref, base_ref, restore, cells, total_cells):
    arrived = arrived_ref[:, : base_ref.shape[0]].astype(jnp.float32)
    total = jnp.sum(arrived, axis=0)
    row = lax.broadcasted_iota(jnp.int32, total.shape, 0)
    marked = (row == cells) | (row == cells + 1)
    power = jnp.sum(jnp.where(marked, total, 0.0), axis=0, keepdims=True)
    peak = jnp.max(jnp.where(row == cells + 2, jnp.max(arrived, axis=0), 0.0), axis=0, keepdims=True)
    integral = total / (1.0 + power / total_cells)
    if restore is not None:
        integral = integral * restore
    sign = jnp.where(low_half(total.shape), half_step, -half_step)
    return integral, base_ref[...] + swapped(integral) * sign, peak


def next_kernel(
    arrived_ref, factor_ref, mask_ref, piece_ref, base_ref, *, cells, total_cells
):
    count = arrived_ref.shape[0]
    padded, wide = base_ref.shape
    row = lax.broadcasted_iota(jnp.int32, (count, wide), 0)
    parts = padded // count
    gathered = [jnp.zeros((count, wide), jnp.float32) for _ in range(parts)]
    for h in range(count):
        extra = arrived_ref[h, padded:].astype(jnp.float32)
        for at in range(parts):
            value = extra[at : at + 1] + extra[parts + at : parts + at + 1]
            gathered[at] = jnp.where(row == h, value, gathered[at])
    base = jnp.concatenate(gathered, 0)
    row = lax.broadcasted_iota(jnp.int32, base.shape, 0)
    base_ref[...] = jnp.where(row < cells, base, 0.0)
    field = advance(arrived_ref, base_ref, None, cells, total_cells)[1]
    write_piece(piece_ref, field, factor_ref, mask_ref, 1.0, cells)


def guarded_kernel(
    arrived_ref, base_ref, factor_ref, mask_ref, piece_ref, restore_ref, *, cells, total_cells
):
    _, field, peak = advance(arrived_ref, base_ref, None, cells, total_cells)
    damping = jnp.where(peak > FAR, SMALL, 1.0)
    restore_ref[...] = jnp.broadcast_to(jnp.where(peak > FAR, LARGE, 1.0), restore_ref.shape)
    write_piece(piece_ref, field, factor_ref, mask_ref, damping, cells)


def last_kernel(arrived_ref, base_ref, restore_ref, row_ref, integral_ref, *, cells, total_cells):
    integral, field, _ = advance(arrived_ref, base_ref, restore_ref[0:1], cells, total_cells)
    times, share, _ = row_ref.shape
    for t in range(times):
        row_ref[t] = field[t * share : (t + 1) * share]
        integral_ref[t] = integral[t * share : (t + 1) * share]


def contract_kernel(pieces_ref, history_ref, *refs, times):
    *extra_refs, out_ref, field_ref, left_ref, terms_ref = refs
    count, padded, wide = pieces_ref.shape
    groups = padded // 8
    shares = count // 2
    orbits = wide // 2
    upper = lax.broadcasted_iota(jnp.int32, (groups, 8, wide), 1) < 4
    for k in range(2):
        for v in range(shares // 2):
            first = pieces_ref[4 * v + k].astype(jnp.float32).reshape(groups, 8, wide)
            second = pieces_ref[4 * v + 2 + k].astype(jnp.float32).reshape(groups, 8, wide)
            even = jnp.where(upper, first, pltpu.roll(second, 4, axis=1))
            odd = jnp.where(upper, pltpu.roll(first, 4, axis=1), second)
            field_ref[k, 0, :, 8 * v : 8 * v + 8, :] = even
            field_ref[k, 1, :, 8 * v : 8 * v + 8, :] = odd
    low = low_half((orbits, wide))
    for pair in range(times):
        blocks = []
        for s in (2 * pair, 2 * pair + 1):
            k, t = divmod(s, times)
            blocks.append(field_ref[k, t % 2, t // 2])
        lanes = slice(pair * wide, (pair + 1) * wide)
        left_ref[:orbits, lanes] = jnp.where(low, blocks[0], swapped(blocks[1])).astype(jnp.bfloat16)
        left_ref[orbits:, lanes] = jnp.where(low, swapped(blocks[0]), blocks[1]).astype(jnp.bfloat16)
    left = left_ref[...]
    depth = left.shape[1]
    sign = jnp.where(low, -1.0, 1.0)
    which = lax.broadcasted_iota(jnp.int32, (orbits, wide), 0) % 4
    marks = [field_ref[k, 1, groups - 1] for k in range(2)]
    power = jnp.sum(jnp.where(which < 2, marks[0] + marks[1], 0.0), axis=0, keepdims=True)
    peak = jnp.max(
        jnp.where(which == 2, jnp.maximum(marks[0], marks[1]), 0.0), axis=0, keepdims=True
    )
    for pair in range(groups):
        moments = [t for t in (2 * pair, 2 * pair + 1) if t < times]
        right = [history_ref[:, t].reshape(depth, wide) for t in moments]
        right = jnp.concatenate(right, -1) if len(right) > 1 else right[0]
        product = jnp.dot(left, right, preferred_element_type=jnp.float32)
        values = []
        for at in range(len(moments)):
            lanes = slice(at * wide, (at + 1) * wide)
            values.append(product[:orbits, lanes] + swapped(product[orbits:, lanes]) * sign)
        if len(moments) < 2:
            values.append(notes(which, 0, power, peak))
        terms_ref[:, 0, pair], terms_ref[:, 1, pair] = packed(*values)
    out_ref[:, :padded] = terms_ref[...].reshape(shares, padded, wide).astype(out_ref.dtype)
    for extra_ref in extra_refs:
        out_ref[:, padded:] = extra_ref[...]


def on_device(g_hist, g_last, integral_last, coupling, step_re, step_im):
    orbits = g_last.shape[0]
    row_count = g_last.shape[1]
    wide = 2 * orbits
    hist_size = lax.axis_size("hist")
    rows_size = lax.axis_size(ROWS)
    fan_out = rows_size // hist_size
    hist_at = lax.axis_index("hist")
    rows_at = lax.axis_index(ROWS)
    plane_at = lax.axis_index(PLANE)
    core_at = lax.axis_index(ROWS[-1])
    total_cells = row_count * rows_size * orbits
    share = orbits // hist_size
    cells = share * row_count
    padded = cells + share
    def exchange(blocks, axes):
        return lax.all_to_all(blocks, axes, split_axis=0, concat_axis=0, tiled=True)

    def my_rows(whole):
        return lax.dynamic_slice_in_dim(whole, hist_at * share, share, 0)

    def as_rows(value):
        value = value.transpose(1, 0, 2).reshape(cells, wide)
        return jnp.pad(value, ((0, padded - cells), (0, 0)))

    def stepped(steps_re, steps_im, rows, integrals):
        shifted = jnp.concatenate(
            [
                rows[..., :orbits] + half_step * integrals[..., orbits:],
                rows[..., orbits:] - half_step * integrals[..., :orbits],
            ],
            -1,
        )
        moved = lax.dot_general(
            jnp.concatenate([steps_re, steps_im], 0),
            shifted,
            (((1,), (1,)), ((), ())),
            precision=lax.Precision.HIGHEST,
            preferred_element_type=jnp.float32,
        ).reshape(2, steps_re.shape[0], rows.shape[0], wide)
        return jnp.concatenate(
            [
                moved[0, ..., :orbits] - moved[1, ..., orbits:],
                moved[0, ..., orbits:] + moved[1, ..., :orbits],
            ],
            -1,
        )

    def base_rows(integral_last):
        by_time = (value.transpose(1, 0, 2) for value in (g_last, integral_last))
        return as_rows(stepped(my_rows(step_re), my_rows(step_im), *by_time))

    def base_chunk():
        def rows_like(steps):
            steps = steps.reshape(hist_size, share, orbits)
            return lax.dynamic_index_in_dim(steps, hist_at % share, 1, keepdims=False)

        def some_times(value):
            value = value.transpose(1, 0, 2)
            start = hist_at // share
            stride = hist_size // share
            return jnp.concatenate(
                [
                    lax.dynamic_slice_in_dim(value, jnp.minimum(start + t, row_count - 1), 1, 0)
                    for t in range(0, padded // share, stride)
                ],
                0,
            )

        chunk = stepped(
            rows_like(step_re), rows_like(step_im), some_times(g_last), some_times(integral_last)
        )
        parts = jnp.concatenate(halves(chunk), 1).astype(jnp.bfloat16)
        return jnp.pad(parts, ((0, 0), (0, hist_size - parts.shape[1]), (0, 0)))

    history = g_hist.transpose(0, 2, 1, 3)
    piece_shape = jax.ShapeDtypeStruct((padded, wide), jnp.bfloat16)
    local_shape = jax.ShapeDtypeStruct((padded, wide), jnp.float32)
    row_shape = jax.ShapeDtypeStruct((row_count, share, wide), jnp.float32)
    sizes = {"cells": cells, "total_cells": total_cells}
    pieces_shape = jax.ShapeDtypeStruct((hist_size, padded, wide), jnp.bfloat16)
    terms = pltpu.VMEM((hist_size // 2, 2, padded // 8, 8, wide), jnp.float32)
    spread, factor, mask = call(
        functools.partial(first_kernel, share=share),
        (pieces_shape, local_shape, local_shape),
        (SCALARS, VECTORS, VECTORS),
        [terms],
    )(
        jnp.stack([rows_at, plane_at, hist_at * fan_out + core_at]).astype(jnp.int32),
        g_last.transpose(1, 0, 2),
        jnp.concatenate([coupling, coupling], -1),
    )
    def contract(pieces, *extra):
        rows = padded + sum(value.shape[1] for value in extra)
        return call(
            functools.partial(contract_kernel, times=row_count),
            jax.ShapeDtypeStruct((hist_size, rows, wide), jnp.bfloat16),
            (VECTORS,) * (2 + len(extra)),
            [
                pltpu.VMEM((fan_out, 2, padded // 8, orbits, wide), jnp.float32),
                pltpu.VMEM((wide, fan_out * row_count * orbits), jnp.bfloat16),
                terms,
            ],
        )(pieces, history, *extra)

    piece = lax.dynamic_index_in_dim(exchange(spread, PLANE), hist_at, 0, keepdims=False)
    for iteration in range(ITERS):
        copies = jnp.broadcast_to(piece[None], (rows_size, padded, wide))
        extra = (base_chunk(),) if iteration == 0 else ()
        sent = contract(exchange(copies, ROWS), *extra)
        if iteration == 0:
            integral_held, sent = lax.optimization_barrier((integral_last, sent))
            base = base_rows(integral_held)
        if iteration < ITERS - 1:
            sent = exchange(sent, PLANE)
        arrived = exchange(sent, "hist")
        if iteration == 0:
            piece, base_moved = call(
                functools.partial(next_kernel, **sizes), (piece_shape, local_shape), (VECTORS,) * 3
            )(arrived, factor, mask)
        elif iteration == 1:
            piece, restore = call(
                functools.partial(guarded_kernel, **sizes),
                (piece_shape, jax.ShapeDtypeStruct((8, wide), jnp.float32)),
                (VECTORS,) * 4,
            )(arrived, base_moved, factor, mask)
        else:
            new_row, new_integral = call(
                functools.partial(last_kernel, **sizes), (row_shape, row_shape), (VECTORS,) * 3
            )(arrived, base, restore)
    return new_row.transpose(1, 0, 2), new_integral.transpose(1, 0, 2)


def solution(mesh):
    split = Mesh(
        mesh.devices.reshape(mesh.shape["hist"], 4, 4, 2), ("hist", "rows_0", "rows_1", "rows_2")
    )
    return jax.shard_map(
        on_device,
        mesh=split,
        in_specs=(
            P("hist", None, ROWS, None),
            P(None, ROWS, None),
            P(None, ROWS, None),
            P(),
            P(),
            P(),
        ),
        out_specs=(P("hist", ROWS, None), P("hist", ROWS, None)),
        check_vma=False,
    )
```

```python
import functools

import jax
import jax.numpy as jnp
from jax import lax
from jax.experimental import pallas as pl
from jax.experimental.pallas import tpu as pltpu
from jax.sharding import Mesh
from jax.sharding import PartitionSpec as P

ITERS = 3
PLANE = ("rows_0", "rows_1")
ROWS = (*PLANE, "rows_2")
SMALL = 2.0**-90
LARGE = 2.0**90
FAR = 2.0**13
SMALL_VMEM = 16 * 2**20

step_size = 0.5
half_step = 0.25


SCALARS = pl.BlockSpec(memory_space=pltpu.SMEM)
VECTORS = pl.BlockSpec(memory_space=pltpu.VMEM)
OUTSIDE = pl.BlockSpec(memory_space=pltpu.HBM)


def call(kernel, shape, specs, scratch=()):
    outs = (VECTORS,) * len(shape) if isinstance(shape, tuple) else VECTORS
    return pl.pallas_call(
        kernel,
        out_shape=shape,
        in_specs=specs,
        out_specs=outs,
        scratch_shapes=list(scratch),
        compiler_params=pltpu.CompilerParams(vmem_limit_bytes=None if OUTSIDE in specs else SMALL_VMEM),
    )


def low_half(shape):
    return lax.broadcasted_iota(jnp.int32, shape, len(shape) - 1) < shape[-1] // 2


def swapped(value):
    return pltpu.roll(value, value.shape[-1] // 2, axis=value.ndim - 1)


def notes(row, first, power, peak):
    high = power.astype(jnp.bfloat16).astype(jnp.float32)
    parts = (high, power - high, peak)
    value = jnp.zeros(row.shape, jnp.float32)
    for at, part in enumerate(parts):
        value = jnp.where(row == first + at, part, value)
    return value


def write_piece(piece_ref, field, factor_ref, mask_ref, damping, cells):
    row = lax.broadcasted_iota(jnp.int32, field.shape, 0)
    square = field * field
    square = square + swapped(square)
    power = jnp.sum(square * mask_ref[...], axis=(0, 1), keepdims=True)
    peak = jnp.max(jnp.where(row < cells, square, 0.0), axis=(0, 1), keepdims=True)
    sigma = factor_ref[...] * (square * damping) * field
    piece_ref[...] = jnp.where(row < cells, sigma, notes(row, cells, power, peak)).astype(
        piece_ref.dtype
    )


def fetch(sources, held, sems):
    copies = [
        pltpu.make_async_copy(source, target, sems.at[at])
        for at, (source, target) in enumerate(zip(sources, held))
    ]
    for copy in copies:
        copy.start()
    for copy in copies:
        copy.wait()


def packed(even, odd):
    even, odd = (value.reshape(-1, 8, value.shape[-1]) for value in (even, odd))
    upper = lax.broadcasted_iota(jnp.int32, even.shape, 1) < 4
    return (
        jnp.where(upper, even, pltpu.roll(odd, 4, axis=1)),
        jnp.where(upper, pltpu.roll(even, 4, axis=1), odd),
    )


def first_kernel(at_ref, *refs, share):
    pieces_ref, factor_ref, mask_ref, terms_ref = refs[2:6]
    rows_ref, coupling_ref = refs[6:8]
    fetch(refs[:2], refs[6:8], refs[8])
    rows_at, plane_at, block_at = at_ref[0], at_ref[1], at_ref[2]
    times, orbits, wide = rows_ref.shape
    count, padded, _ = pieces_ref.shape
    row = lax.broadcasted_iota(jnp.int32, (orbits, wide), 0)
    lane = lax.broadcasted_iota(jnp.int32, (orbits, wide), 1)
    own = coupling_ref[...] * step_size
    own = jnp.concatenate([own, own], -1)
    power = jnp.zeros((orbits, wide), jnp.float32)
    peak = jnp.zeros((orbits, wide), jnp.float32)
    values = []
    for t in range(times):
        field = rows_ref[t]
        square = field * field
        square = square + swapped(square)
        power = power + jnp.where(lane == row, square, 0.0)
        peak = jnp.maximum(peak, square)
        scaled = jnp.where(rows_at == 0, own * 0.5, own) if t == 0 else own
        values.append(scaled * square * field)
    power = jnp.sum(power, axis=(0, 1), keepdims=True)
    peak = jnp.max(peak, axis=(0, 1), keepdims=True)
    values.append(notes(row % share, 0, jnp.where(row < share, power, 0.0), peak))
    for pair in range(padded // 8):
        terms_ref[:, 0, pair], terms_ref[:, 1, pair] = packed(*values[2 * pair : 2 * pair + 2])
    pieces_ref[...] = terms_ref[...].reshape(count, padded, wide).astype(pieces_ref.dtype)

    start = pl.multiple_of(plane_at // 2 * 8, 8)
    mine = coupling_ref[pl.ds(start, 8), :] * step_size
    mine = jnp.concatenate([mine, mine], -1)
    turned = pltpu.roll(mine, 4, axis=0)
    row = lax.broadcasted_iota(jnp.int32, mine.shape, 0)
    lane = lax.broadcasted_iota(jnp.int32, mine.shape, 1)
    upper = row < share
    factor = jnp.where(upper == (plane_at % 2 == 0), mine, turned)
    mask = jnp.where(lane == plane_at * share + row % share, 1.0, 0.0)
    for group in range(padded // 8):
        scaled, kept = factor, mask
        if group == 0:
            scaled = jnp.where(upper & (block_at == 0), factor * 0.5, factor)
        if 2 * group + 1 == times:
            scaled, kept = jnp.where(upper, factor, 0.0), jnp.where(upper, mask, 0.0)
        factor_ref[8 * group : 8 * group + 8, :] = scaled
        mask_ref[8 * group : 8 * group + 8, :] = kept


def base_kernel(at_ref, *refs):
    base_ref, extra_ref, terms_ref = refs[4:7]
    rows_ref, integrals_ref, step_re_ref, step_im_ref = refs[7:11]
    fetch(refs[:4], refs[7:11], refs[11])
    hist_at = at_ref[0]
    times, orbits, wide = rows_ref.shape
    count = extra_ref.shape[0]
    padded = base_ref.shape[0]
    low = low_half((orbits, wide))
    sign = jnp.where(low, half_step, -half_step)
    turn = jnp.where(low, -1.0, 1.0)
    shifted = [rows_ref[t] + swapped(integrals_ref[t]) * sign for t in range(times)]
    steps = jnp.concatenate([step_re_ref[...], step_im_ref[...]], 0)
    moved = jnp.dot(
        steps,
        jnp.concatenate(shifted, -1),
        precision=lax.Precision.HIGHEST,
        preferred_element_type=jnp.float32,
    )
    values = []
    for t in range(times):
        lanes = slice(t * wide, (t + 1) * wide)
        values.append(moved[:orbits, lanes] + swapped(moved[orbits:, lanes]) * turn)
    values.append(jnp.zeros((orbits, wide), jnp.float32))
    for pair in range(padded // 8):
        terms_ref[:, 0, pair], terms_ref[:, 1, pair] = packed(*values[2 * pair : 2 * pair + 2])
    base_ref[...] = terms_ref[hist_at // 2, hist_at % 2].reshape(padded, wide)
    parts = padded // count
    sub = lax.broadcasted_iota(jnp.int32, (8, wide), 0)
    row = lax.broadcasted_iota(jnp.int32, extra_ref.shape[1:], 0)
    for share in range(count):
        extra = jnp.zeros(row.shape, jnp.float32)
        for at in range(parts):
            group = terms_ref[share // 2, share % 2, at * (count // 8) + hist_at // 8]
            value = jnp.sum(jnp.where(sub == hist_at % 8, group, 0.0), axis=0, keepdims=True)
            high = value.astype(jnp.bfloat16).astype(jnp.float32)
            extra = jnp.where(row == at, high, extra)
            extra = jnp.where(row == parts + at, value - high, extra)
        extra_ref[share] = extra.astype(extra_ref.dtype)


def advance(arrived_ref, base_ref, restore, cells, total_cells):
    arrived = arrived_ref[:, : base_ref.shape[0]].astype(jnp.float32)
    total = jnp.sum(arrived, axis=0)
    row = lax.broadcasted_iota(jnp.int32, total.shape, 0)
    marked = (row == cells) | (row == cells + 1)
    power = jnp.sum(jnp.where(marked, total, 0.0), axis=0, keepdims=True)
    peak = jnp.max(jnp.where(row == cells + 2, jnp.max(arrived, axis=0), 0.0), axis=0, keepdims=True)
    integral = total / (1.0 + power / total_cells)
    if restore is not None:
        integral = integral * restore
    sign = jnp.where(low_half(total.shape), half_step, -half_step)
    return integral, base_ref[...] + swapped(integral) * sign, peak


def next_kernel(
    arrived_ref, factor_ref, mask_ref, piece_ref, base_ref, *, cells, total_cells
):
    count = arrived_ref.shape[0]
    padded, wide = base_ref.shape
    row = lax.broadcasted_iota(jnp.int32, (count, wide), 0)
    parts = padded // count
    gathered = [jnp.zeros((count, wide), jnp.float32) for _ in range(parts)]
    for h in range(count):
        extra = arrived_ref[h, padded:].astype(jnp.float32)
        for at in range(parts):
            value = extra[at : at + 1] + extra[parts + at : parts + at + 1]
            gathered[at] = jnp.where(row == h, value, gathered[at])
    base = jnp.concatenate(gathered, 0)
    row = lax.broadcasted_iota(jnp.int32, base.shape, 0)
    base_ref[...] = jnp.where(row < cells, base, 0.0)
    field = advance(arrived_ref, base_ref, None, cells, total_cells)[1]
    write_piece(piece_ref, field, factor_ref, mask_ref, 1.0, cells)


def guarded_kernel(
    arrived_ref, base_ref, factor_ref, mask_ref, piece_ref, restore_ref, *, cells, total_cells
):
    _, field, peak = advance(arrived_ref, base_ref, None, cells, total_cells)
    damping = jnp.where(peak > FAR, SMALL, 1.0)
    restore_ref[...] = jnp.broadcast_to(jnp.where(peak > FAR, LARGE, 1.0), restore_ref.shape)
    write_piece(piece_ref, field, factor_ref, mask_ref, damping, cells)


def last_kernel(arrived_ref, base_ref, restore_ref, row_ref, integral_ref, *, cells, total_cells):
    integral, field, _ = advance(arrived_ref, base_ref, restore_ref[0:1], cells, total_cells)
    times, share, _ = row_ref.shape
    for t in range(times):
        row_ref[t] = field[t * share : (t + 1) * share]
        integral_ref[t] = integral[t * share : (t + 1) * share]


def contract_kernel(pieces_ref, history_ref, *refs, times):
    *extra_refs, out_ref, field_ref, left_ref, terms_ref = refs
    count, padded, wide = pieces_ref.shape
    groups = padded // 8
    shares = count // 2
    orbits = wide // 2
    upper = lax.broadcasted_iota(jnp.int32, (groups, 8, wide), 1) < 4
    for k in range(2):
        for v in range(shares // 2):
            first = pieces_ref[4 * v + k].astype(jnp.float32).reshape(groups, 8, wide)
            second = pieces_ref[4 * v + 2 + k].astype(jnp.float32).reshape(groups, 8, wide)
            even = jnp.where(upper, first, pltpu.roll(second, 4, axis=1))
            odd = jnp.where(upper, pltpu.roll(first, 4, axis=1), second)
            field_ref[k, 0, :, 8 * v : 8 * v + 8, :] = even
            field_ref[k, 1, :, 8 * v : 8 * v + 8, :] = odd
    low = low_half((orbits, wide))
    for pair in range(times):
        blocks = []
        for s in (2 * pair, 2 * pair + 1):
            k, t = divmod(s, times)
            blocks.append(field_ref[k, t % 2, t // 2])
        lanes = slice(pair * wide, (pair + 1) * wide)
        left_ref[:orbits, lanes] = jnp.where(low, blocks[0], swapped(blocks[1])).astype(jnp.bfloat16)
        left_ref[orbits:, lanes] = jnp.where(low, swapped(blocks[0]), blocks[1]).astype(jnp.bfloat16)
    left = left_ref[...]
    depth = left.shape[1]
    sign = jnp.where(low, -1.0, 1.0)
    which = lax.broadcasted_iota(jnp.int32, (orbits, wide), 0) % 4
    marks = [field_ref[k, 1, groups - 1] for k in range(2)]
    power = jnp.sum(jnp.where(which < 2, marks[0] + marks[1], 0.0), axis=0, keepdims=True)
    peak = jnp.max(
        jnp.where(which == 2, jnp.maximum(marks[0], marks[1]), 0.0), axis=0, keepdims=True
    )
    for pair in range(groups):
        moments = [t for t in (2 * pair, 2 * pair + 1) if t < times]
        right = [history_ref[:, t].reshape(depth, wide) for t in moments]
        right = jnp.concatenate(right, -1) if len(right) > 1 else right[0]
        product = jnp.dot(left, right, preferred_element_type=jnp.float32)
        values = []
        for at in range(len(moments)):
            lanes = slice(at * wide, (at + 1) * wide)
            values.append(product[:orbits, lanes] + swapped(product[orbits:, lanes]) * sign)
        if len(moments) < 2:
            values.append(notes(which, 0, power, peak))
        terms_ref[:, 0, pair], terms_ref[:, 1, pair] = packed(*values)
    out_ref[:, :padded] = terms_ref[...].reshape(shares, padded, wide).astype(out_ref.dtype)
    for extra_ref in extra_refs:
        out_ref[:, padded:] = extra_ref[...]


def on_device(g_hist, g_last, integral_last, coupling, step_re, step_im):
    orbits = g_last.shape[0]
    row_count = g_last.shape[1]
    wide = 2 * orbits
    hist_size = lax.axis_size("hist")
    rows_size = lax.axis_size(ROWS)
    fan_out = rows_size // hist_size
    hist_at = lax.axis_index("hist")
    rows_at = lax.axis_index(ROWS)
    plane_at = lax.axis_index(PLANE)
    core_at = lax.axis_index(ROWS[-1])
    total_cells = row_count * rows_size * orbits
    share = orbits // hist_size
    cells = share * row_count
    padded = cells + share
    def exchange(blocks, axes):
        return lax.all_to_all(blocks, axes, split_axis=0, concat_axis=0, tiled=True)

    history = g_hist.transpose(0, 2, 1, 3)
    piece_shape = jax.ShapeDtypeStruct((padded, wide), jnp.bfloat16)
    local_shape = jax.ShapeDtypeStruct((padded, wide), jnp.float32)
    row_shape = jax.ShapeDtypeStruct((row_count, share, wide), jnp.float32)
    sizes = {"cells": cells, "total_cells": total_cells}
    pieces_shape = jax.ShapeDtypeStruct((hist_size, padded, wide), jnp.bfloat16)
    terms = pltpu.VMEM((hist_size // 2, 2, padded // 8, 8, wide), jnp.float32)
    by_time = [pltpu.VMEM((row_count, orbits, wide), jnp.float32)] * 2
    square = pltpu.VMEM((orbits, orbits), jnp.float32)
    spread, factor, mask = call(
        functools.partial(first_kernel, share=share),
        (pieces_shape, local_shape, local_shape),
        (SCALARS, OUTSIDE, OUTSIDE),
        [terms, *by_time[:1], square, pltpu.SemaphoreType.DMA((2,))],
    )(
        jnp.stack([rows_at, plane_at, hist_at * fan_out + core_at]).astype(jnp.int32),
        g_last.transpose(1, 0, 2),
        coupling,
    )
    integral_held, spread = lax.optimization_barrier((integral_last, spread))
    base, extra = call(
        base_kernel,
        (local_shape, jax.ShapeDtypeStruct((hist_size, 16, wide), jnp.bfloat16)),
        (SCALARS, *(OUTSIDE,) * 4),
        [terms, *by_time, square, square, pltpu.SemaphoreType.DMA((4,))],
    )(
        hist_at.astype(jnp.int32)[None],
        g_last.transpose(1, 0, 2),
        integral_held.transpose(1, 0, 2),
        step_re,
        step_im,
    )

    def contract(pieces, *extra):
        rows = padded + sum(value.shape[1] for value in extra)
        return call(
            functools.partial(contract_kernel, times=row_count),
            jax.ShapeDtypeStruct((hist_size, rows, wide), jnp.bfloat16),
            (VECTORS,) * (2 + len(extra)),
            [
                pltpu.VMEM((fan_out, 2, padded // 8, orbits, wide), jnp.float32),
                pltpu.VMEM((wide, fan_out * row_count * orbits), jnp.bfloat16),
                terms,
            ],
        )(pieces, history, *extra)

    piece = lax.dynamic_index_in_dim(exchange(spread, PLANE), hist_at, 0, keepdims=False)
    piece, base, extra = lax.optimization_barrier((piece, base, extra))
    for iteration in range(ITERS):
        copies = jnp.broadcast_to(piece[None], (rows_size, padded, wide))
        pieces = exchange(copies, ROWS)
        sent = contract(pieces, extra) if iteration == 0 else contract(pieces)
        if iteration < ITERS - 1:
            sent = exchange(sent, PLANE)
        arrived = exchange(sent, "hist")
        if iteration == 0:
            piece, base_moved = call(
                functools.partial(next_kernel, **sizes), (piece_shape, local_shape), (VECTORS,) * 3
            )(arrived, factor, mask)
        elif iteration == 1:
            piece, restore = call(
                functools.partial(guarded_kernel, **sizes),
                (piece_shape, jax.ShapeDtypeStruct((8, wide), jnp.float32)),
                (VECTORS,) * 4,
            )(arrived, base_moved, factor, mask)
        else:
            new_row, new_integral = call(
                functools.partial(last_kernel, **sizes), (row_shape, row_shape), (VECTORS,) * 3
            )(arrived, base, restore)
    return new_row.transpose(1, 0, 2), new_integral.transpose(1, 0, 2)


def solution(mesh):
    split = Mesh(
        mesh.devices.reshape(mesh.shape["hist"], 4, 4, 2), ("hist", "rows_0", "rows_1", "rows_2")
    )
    return jax.shard_map(
        on_device,
        mesh=split,
        in_specs=(
            P("hist", None, ROWS, None),
            P(None, ROWS, None),
            P(None, ROWS, None),
            P(),
            P(),
            P(),
        ),
        out_specs=(P("hist", ROWS, None), P("hist", ROWS, None)),
        check_vma=False,
    )
```

```python
import functools

import jax
import jax.numpy as jnp
from jax import lax
from jax.experimental import pallas as pl
from jax.experimental.pallas import tpu as pltpu
from jax.sharding import Mesh
from jax.sharding import PartitionSpec as P

ITERS = 3
PLANE = ("rows_0", "rows_1")
ROWS = (*PLANE, "rows_2")
SMALL = 2.0**-90
LARGE = 2.0**90
FAR = 2.0**13
SMALL_VMEM = 16 * 2**20

step_size = 0.5
half_step = 0.25


VECTORS = pl.BlockSpec(memory_space=pltpu.VMEM)
OUTSIDE = pl.BlockSpec(memory_space=pltpu.HBM)


def call(kernel, shape, specs, scratch=()):
    outs = (VECTORS,) * len(shape) if isinstance(shape, tuple) else VECTORS
    return pl.pallas_call(
        kernel,
        out_shape=shape,
        in_specs=specs,
        out_specs=outs,
        scratch_shapes=list(scratch),
        compiler_params=pltpu.CompilerParams(vmem_limit_bytes=SMALL_VMEM),
    )


def far(value):
    return pltpu.with_memory_space_constraint(value, pltpu.HBM)


def low_half(shape):
    return lax.broadcasted_iota(jnp.int32, shape, len(shape) - 1) < shape[-1] // 2


def swapped(value):
    return pltpu.roll(value, value.shape[-1] // 2, axis=value.ndim - 1)


def notes(row, first, power, peak):
    high = power.astype(jnp.bfloat16).astype(jnp.float32)
    parts = (high, power - high, peak)
    value = jnp.zeros(row.shape, jnp.float32)
    for at, part in enumerate(parts):
        value = jnp.where(row == first + at, part, value)
    return value


def write_piece(piece_ref, field, factor_ref, mask_ref, damping, cells):
    row = lax.broadcasted_iota(jnp.int32, field.shape, 0)
    square = field * field
    square = square + swapped(square)
    power = jnp.sum(square * mask_ref[...], axis=(0, 1), keepdims=True)
    peak = jnp.max(jnp.where(row < cells, square, 0.0), axis=(0, 1), keepdims=True)
    sigma = factor_ref[...] * (square * damping) * field
    piece_ref[...] = jnp.where(row < cells, sigma, notes(row, cells, power, peak)).astype(
        piece_ref.dtype
    )


def fetch(sources, held, sems):
    copies = [
        pltpu.make_async_copy(source, target, sems.at[at])
        for at, (source, target) in enumerate(zip(sources, held))
    ]
    for copy in copies:
        copy.start()
    for copy in copies:
        copy.wait()


def packed(even, odd):
    even, odd = (value.reshape(-1, 8, value.shape[-1]) for value in (even, odd))
    upper = lax.broadcasted_iota(jnp.int32, even.shape, 1) < 4
    return (
        jnp.where(upper, even, pltpu.roll(odd, 4, axis=1)),
        jnp.where(upper, pltpu.roll(even, 4, axis=1), odd),
    )


def first_kernel(*refs, share):
    pieces_ref, factor_ref, mask_ref, terms_ref = refs[2:6]
    rows_ref, coupling_ref = refs[6:8]
    fetch(refs[:2], refs[6:8], refs[8])
    rows_at = lax.axis_index(ROWS)
    plane_at = lax.axis_index(PLANE)
    block_at = lax.axis_index("hist") * lax.axis_size(ROWS[-1]) + lax.axis_index(ROWS[-1])
    times, orbits, wide = rows_ref.shape
    count, padded, _ = pieces_ref.shape
    row = lax.broadcasted_iota(jnp.int32, (orbits, wide), 0)
    lane = lax.broadcasted_iota(jnp.int32, (orbits, wide), 1)
    own = coupling_ref[...] * step_size
    own = jnp.concatenate([own, own], -1)
    power = jnp.zeros((orbits, wide), jnp.float32)
    peak = jnp.zeros((orbits, wide), jnp.float32)
    values = []
    for t in range(times):
        field = rows_ref[t]
        square = field * field
        square = square + swapped(square)
        power = power + jnp.where(lane == row, square, 0.0)
        peak = jnp.maximum(peak, square)
        scaled = jnp.where(rows_at == 0, own * 0.5, own) if t == 0 else own
        values.append(scaled * square * field)
    power = jnp.sum(power, axis=(0, 1), keepdims=True)
    peak = jnp.max(peak, axis=(0, 1), keepdims=True)
    values.append(notes(row % share, 0, jnp.where(row < share, power, 0.0), peak))
    for pair in range(padded // 8):
        terms_ref[:, 0, pair], terms_ref[:, 1, pair] = packed(*values[2 * pair : 2 * pair + 2])
    pieces_ref[...] = terms_ref[...].reshape(count, padded, wide).astype(pieces_ref.dtype)

    start = pl.multiple_of(plane_at // 2 * 8, 8)
    mine = coupling_ref[pl.ds(start, 8), :] * step_size
    mine = jnp.concatenate([mine, mine], -1)
    turned = pltpu.roll(mine, 4, axis=0)
    row = lax.broadcasted_iota(jnp.int32, mine.shape, 0)
    lane = lax.broadcasted_iota(jnp.int32, mine.shape, 1)
    upper = row < share
    factor = jnp.where(upper == (plane_at % 2 == 0), mine, turned)
    mask = jnp.where(lane == plane_at * share + row % share, 1.0, 0.0)
    for group in range(padded // 8):
        scaled, kept = factor, mask
        if group == 0:
            scaled = jnp.where(upper & (block_at == 0), factor * 0.5, factor)
        if 2 * group + 1 == times:
            scaled, kept = jnp.where(upper, factor, 0.0), jnp.where(upper, mask, 0.0)
        factor_ref[8 * group : 8 * group + 8, :] = scaled
        mask_ref[8 * group : 8 * group + 8, :] = kept


def base_kernel(*refs):
    base_ref, extra_ref, terms_ref = refs[4:7]
    rows_ref, integrals_ref, step_re_ref, step_im_ref = refs[7:11]
    fetch(refs[:4], refs[7:11], refs[11])
    hist_at = lax.axis_index("hist")
    times, orbits, wide = rows_ref.shape
    count = extra_ref.shape[0]
    padded = base_ref.shape[0]
    low = low_half((orbits, wide))
    sign = jnp.where(low, half_step, -half_step)
    turn = jnp.where(low, -1.0, 1.0)
    shifted = [rows_ref[t] + swapped(integrals_ref[t]) * sign for t in range(times)]
    steps = jnp.concatenate([step_re_ref[...], step_im_ref[...]], 0)
    moved = jnp.dot(
        steps,
        jnp.concatenate(shifted, -1),
        precision=lax.Precision.HIGHEST,
        preferred_element_type=jnp.float32,
    )
    values = []
    for t in range(times):
        lanes = slice(t * wide, (t + 1) * wide)
        values.append(moved[:orbits, lanes] + swapped(moved[orbits:, lanes]) * turn)
    values.append(jnp.zeros((orbits, wide), jnp.float32))
    for pair in range(padded // 8):
        terms_ref[:, 0, pair], terms_ref[:, 1, pair] = packed(*values[2 * pair : 2 * pair + 2])
    base_ref[...] = terms_ref[hist_at // 2, hist_at % 2].reshape(padded, wide)
    parts = padded // count
    sub = lax.broadcasted_iota(jnp.int32, (8, wide), 0)
    row = lax.broadcasted_iota(jnp.int32, extra_ref.shape[1:], 0)
    for share in range(count):
        extra = jnp.zeros(row.shape, jnp.float32)
        for at in range(parts):
            group = terms_ref[share // 2, share % 2, at * (count // 8) + hist_at // 8]
            value = jnp.sum(jnp.where(sub == hist_at % 8, group, 0.0), axis=0, keepdims=True)
            high = value.astype(jnp.bfloat16).astype(jnp.float32)
            extra = jnp.where(row == at, high, extra)
            extra = jnp.where(row == parts + at, value - high, extra)
        extra_ref[share] = extra.astype(extra_ref.dtype)


def advance(arrived_ref, base_ref, restore, cells, total_cells):
    arrived = arrived_ref[:, : base_ref.shape[0]].astype(jnp.float32)
    total = jnp.sum(arrived, axis=0)
    row = lax.broadcasted_iota(jnp.int32, total.shape, 0)
    marked = (row == cells) | (row == cells + 1)
    power = jnp.sum(jnp.where(marked, total, 0.0), axis=0, keepdims=True)
    peak = jnp.max(jnp.where(row == cells + 2, jnp.max(arrived, axis=0), 0.0), axis=0, keepdims=True)
    integral = total / (1.0 + power / total_cells)
    if restore is not None:
        integral = integral * restore
    sign = jnp.where(low_half(total.shape), half_step, -half_step)
    return integral, base_ref[...] + swapped(integral) * sign, peak


def next_kernel(
    arrived_ref, factor_ref, mask_ref, piece_ref, base_ref, *, cells, total_cells
):
    count = arrived_ref.shape[0]
    padded, wide = base_ref.shape
    row = lax.broadcasted_iota(jnp.int32, (count, wide), 0)
    parts = padded // count
    gathered = [jnp.zeros((count, wide), jnp.float32) for _ in range(parts)]
    for h in range(count):
        extra = arrived_ref[h, padded:].astype(jnp.float32)
        for at in range(parts):
            value = extra[at : at + 1] + extra[parts + at : parts + at + 1]
            gathered[at] = jnp.where(row == h, value, gathered[at])
    base = jnp.concatenate(gathered, 0)
    row = lax.broadcasted_iota(jnp.int32, base.shape, 0)
    base_ref[...] = jnp.where(row < cells, base, 0.0)
    field = advance(arrived_ref, base_ref, None, cells, total_cells)[1]
    write_piece(piece_ref, field, factor_ref, mask_ref, 1.0, cells)


def guarded_kernel(
    arrived_ref, base_ref, factor_ref, mask_ref, piece_ref, restore_ref, *, cells, total_cells
):
    _, field, peak = advance(arrived_ref, base_ref, None, cells, total_cells)
    damping = jnp.where(peak > FAR, SMALL, 1.0)
    restore_ref[...] = jnp.broadcast_to(jnp.where(peak > FAR, LARGE, 1.0), restore_ref.shape)
    write_piece(piece_ref, field, factor_ref, mask_ref, damping, cells)


def last_kernel(arrived_ref, base_ref, restore_ref, row_ref, integral_ref, *, cells, total_cells):
    integral, field, _ = advance(arrived_ref, base_ref, restore_ref[0:1], cells, total_cells)
    times, share, _ = row_ref.shape
    for t in range(times):
        row_ref[t] = field[t * share : (t + 1) * share]
        integral_ref[t] = integral[t * share : (t + 1) * share]


def contract_kernel(pieces_ref, history_ref, *refs, times):
    *extra_refs, out_ref, field_ref, left_ref, terms_ref = refs
    count, padded, wide = pieces_ref.shape
    groups = padded // 8
    shares = count // 2
    orbits = wide // 2
    upper = lax.broadcasted_iota(jnp.int32, (groups, 8, wide), 1) < 4
    for k in range(2):
        for v in range(shares // 2):
            first = pieces_ref[4 * v + k].astype(jnp.float32).reshape(groups, 8, wide)
            second = pieces_ref[4 * v + 2 + k].astype(jnp.float32).reshape(groups, 8, wide)
            even = jnp.where(upper, first, pltpu.roll(second, 4, axis=1))
            odd = jnp.where(upper, pltpu.roll(first, 4, axis=1), second)
            field_ref[k, 0, :, 8 * v : 8 * v + 8, :] = even
            field_ref[k, 1, :, 8 * v : 8 * v + 8, :] = odd
    low = low_half((orbits, wide))
    for pair in range(times):
        blocks = []
        for s in (2 * pair, 2 * pair + 1):
            k, t = divmod(s, times)
            blocks.append(field_ref[k, t % 2, t // 2])
        lanes = slice(pair * wide, (pair + 1) * wide)
        left_ref[:orbits, lanes] = jnp.where(low, blocks[0], swapped(blocks[1])).astype(jnp.bfloat16)
        left_ref[orbits:, lanes] = jnp.where(low, swapped(blocks[0]), blocks[1]).astype(jnp.bfloat16)
    left = left_ref[...]
    depth = left.shape[1]
    sign = jnp.where(low, -1.0, 1.0)
    which = lax.broadcasted_iota(jnp.int32, (orbits, wide), 0) % 4
    marks = [field_ref[k, 1, groups - 1] for k in range(2)]
    power = jnp.sum(jnp.where(which < 2, marks[0] + marks[1], 0.0), axis=0, keepdims=True)
    peak = jnp.max(
        jnp.where(which == 2, jnp.maximum(marks[0], marks[1]), 0.0), axis=0, keepdims=True
    )
    for pair in range(groups):
        moments = [t for t in (2 * pair, 2 * pair + 1) if t < times]
        right = [history_ref[:, t].reshape(depth, wide) for t in moments]
        right = jnp.concatenate(right, -1) if len(right) > 1 else right[0]
        product = jnp.dot(left, right, preferred_element_type=jnp.float32)
        values = []
        for at in range(len(moments)):
            lanes = slice(at * wide, (at + 1) * wide)
            values.append(product[:orbits, lanes] + swapped(product[orbits:, lanes]) * sign)
        if len(moments) < 2:
            values.append(notes(which, 0, power, peak))
        terms_ref[:, 0, pair], terms_ref[:, 1, pair] = packed(*values)
    out_ref[:, :padded] = terms_ref[...].reshape(shares, padded, wide).astype(out_ref.dtype)
    for extra_ref in extra_refs:
        out_ref[:, padded:] = extra_ref[...]


def on_device(g_hist, g_last, integral_last, coupling, step_re, step_im):
    orbits = g_last.shape[0]
    row_count = g_last.shape[1]
    wide = 2 * orbits
    hist_size = lax.axis_size("hist")
    rows_size = lax.axis_size(ROWS)
    fan_out = rows_size // hist_size
    hist_at = lax.axis_index("hist")
    total_cells = row_count * rows_size * orbits
    share = orbits // hist_size
    cells = share * row_count
    padded = cells + share
    def exchange(blocks, axes):
        return lax.all_to_all(blocks, axes, split_axis=0, concat_axis=0, tiled=True)

    history = g_hist.transpose(0, 2, 1, 3)
    piece_shape = jax.ShapeDtypeStruct((padded, wide), jnp.bfloat16)
    local_shape = jax.ShapeDtypeStruct((padded, wide), jnp.float32)
    row_shape = jax.ShapeDtypeStruct((row_count, share, wide), jnp.float32)
    sizes = {"cells": cells, "total_cells": total_cells}
    pieces_shape = jax.ShapeDtypeStruct((hist_size, padded, wide), jnp.bfloat16)
    terms = pltpu.VMEM((hist_size // 2, 2, padded // 8, 8, wide), jnp.float32)
    by_time = [pltpu.VMEM((row_count, orbits, wide), jnp.float32)] * 2
    square = pltpu.VMEM((orbits, orbits), jnp.float32)
    spread, factor, mask = call(
        functools.partial(first_kernel, share=share),
        (pieces_shape, local_shape, local_shape),
        (OUTSIDE,) * 2,
        [terms, *by_time[:1], square, pltpu.SemaphoreType.DMA((2,))],
    )(
        far(g_last.transpose(1, 0, 2)),
        far(coupling),
    )
    integral_held, spread = lax.optimization_barrier((integral_last, spread))
    base, extra = call(
        base_kernel,
        (local_shape, jax.ShapeDtypeStruct((hist_size, 8, wide), jnp.bfloat16)),
        (OUTSIDE,) * 4,
        [terms, *by_time, square, square, pltpu.SemaphoreType.DMA((4,))],
    )(
        far(g_last.transpose(1, 0, 2)),
        far(integral_held.transpose(1, 0, 2)),
        far(step_re),
        far(step_im),
    )

    def contract(*operands):
        rows = padded + sum(value.shape[1] for value in operands[2:])
        return call(
            functools.partial(contract_kernel, times=row_count),
            jax.ShapeDtypeStruct((hist_size, rows, wide), jnp.bfloat16),
            (VECTORS,) * len(operands),
            [
                pltpu.VMEM((fan_out, 2, padded // 8, orbits, wide), jnp.float32),
                pltpu.VMEM((wide, fan_out * row_count * orbits), jnp.bfloat16),
                terms,
            ],
        )(*operands)

    piece = lax.dynamic_index_in_dim(exchange(spread, PLANE), hist_at, 0, keepdims=False)
    piece, base, extra = lax.optimization_barrier((piece, base, extra))
    for iteration in range(ITERS):
        copies = jnp.broadcast_to(piece[None], (rows_size, padded, wide))
        pieces = exchange(copies, ROWS)
        sent = contract(pieces, history, *([extra] if iteration == 0 else []))
        if iteration < ITERS - 1:
            sent = exchange(sent, PLANE)
        arrived = exchange(sent, "hist")
        if iteration == 0:
            piece, base_moved = call(
                functools.partial(next_kernel, **sizes), (piece_shape, local_shape), (VECTORS,) * 3
            )(arrived, factor, mask)
        elif iteration == 1:
            piece, restore = call(
                functools.partial(guarded_kernel, **sizes),
                (piece_shape, jax.ShapeDtypeStruct((8, wide), jnp.float32)),
                (VECTORS,) * 4,
            )(arrived, base_moved, factor, mask)
        else:
            new_row, new_integral = call(
                functools.partial(last_kernel, **sizes), (row_shape, row_shape), (VECTORS,) * 3
            )(arrived, base, restore)
    return new_row.transpose(1, 0, 2), new_integral.transpose(1, 0, 2)


def solution(mesh):
    split = Mesh(
        mesh.devices.reshape(mesh.shape["hist"], 4, 4, 2), ("hist", "rows_0", "rows_1", "rows_2")
    )
    return jax.shard_map(
        on_device,
        mesh=split,
        in_specs=(
            P("hist", None, ROWS, None),
            P(None, ROWS, None),
            P(None, ROWS, None),
            P(),
            P(),
            P(),
        ),
        out_specs=(P("hist", ROWS, None), P("hist", ROWS, None)),
        check_vma=False,
    )
```

```python
import functools

import jax
import jax.numpy as jnp
from jax import lax
from jax.experimental import pallas as pl
from jax.experimental.pallas import tpu as pltpu
from jax.sharding import Mesh
from jax.sharding import PartitionSpec as P

ITERS = 3
PLANE = ("rows_0", "rows_1")
ROWS = (*PLANE, "rows_2")
SMALL = 2.0**-90
LARGE = 2.0**90
FAR = 2.0**13
SMALL_VMEM = 16 * 2**20

step_size = 0.5
half_step = 0.25


VECTORS = pl.BlockSpec(memory_space=pltpu.VMEM)
OUTSIDE = pl.BlockSpec(memory_space=pltpu.HBM)


def call(kernel, shape, specs, scratch=(), cost=None):
    outs = (VECTORS,) * len(shape) if isinstance(shape, tuple) else VECTORS
    return pl.pallas_call(
        kernel,
        out_shape=shape,
        in_specs=specs,
        out_specs=outs,
        scratch_shapes=list(scratch),
        cost_estimate=cost,
        compiler_params=pltpu.CompilerParams(vmem_limit_bytes=SMALL_VMEM),
    )


def far(value):
    return pltpu.with_memory_space_constraint(value, pltpu.HBM)


def low_half(shape):
    return lax.broadcasted_iota(jnp.int32, shape, len(shape) - 1) < shape[-1] // 2


def swapped(value):
    return pltpu.roll(value, value.shape[-1] // 2, axis=value.ndim - 1)


def notes(row, first, power, peak):
    high = power.astype(jnp.bfloat16).astype(jnp.float32)
    parts = (high, power - high, peak)
    value = jnp.zeros(row.shape, jnp.float32)
    for at, part in enumerate(parts):
        value = jnp.where(row == first + at, part, value)
    return value


def write_piece(piece_ref, field, factor_ref, mask_ref, damping, cells):
    row = lax.broadcasted_iota(jnp.int32, field.shape, 0)
    square = field * field
    square = square + swapped(square)
    power = jnp.sum(square * mask_ref[...], axis=(0, 1), keepdims=True)
    peak = jnp.max(jnp.where(row < cells, square, 0.0), axis=(0, 1), keepdims=True)
    sigma = factor_ref[...] * (square * damping) * field
    piece_ref[...] = jnp.where(row < cells, sigma, notes(row, cells, power, peak)).astype(
        piece_ref.dtype
    )


def fetch(sources, held, sems):
    copies = [
        pltpu.make_async_copy(source, target, sems.at[at])
        for at, (source, target) in enumerate(zip(sources, held))
    ]
    for copy in copies:
        copy.start()
    for copy in copies:
        copy.wait()


def packed(even, odd):
    even, odd = (value.reshape(-1, 8, value.shape[-1]) for value in (even, odd))
    upper = lax.broadcasted_iota(jnp.int32, even.shape, 1) < 4
    return (
        jnp.where(upper, even, pltpu.roll(odd, 4, axis=1)),
        jnp.where(upper, pltpu.roll(even, 4, axis=1), odd),
    )


def first_kernel(*refs, share):
    pieces_ref, factor_ref, mask_ref, terms_ref = refs[2:6]
    rows_ref, coupling_ref = refs[6:8]
    fetch(refs[:2], refs[6:8], refs[8])
    rows_at = lax.axis_index(ROWS)
    plane_at = lax.axis_index(PLANE)
    block_at = lax.axis_index("hist") * lax.axis_size(ROWS[-1]) + lax.axis_index(ROWS[-1])
    times, orbits, wide = rows_ref.shape
    count, padded, _ = pieces_ref.shape
    row = lax.broadcasted_iota(jnp.int32, (orbits, wide), 0)
    lane = lax.broadcasted_iota(jnp.int32, (orbits, wide), 1)
    own = coupling_ref[...] * step_size
    own = jnp.concatenate([own, own], -1)
    power = jnp.zeros((orbits, wide), jnp.float32)
    peak = jnp.zeros((orbits, wide), jnp.float32)
    values = []
    for t in range(times):
        field = rows_ref[t]
        square = field * field
        square = square + swapped(square)
        power = power + jnp.where(lane == row, square, 0.0)
        peak = jnp.maximum(peak, square)
        scaled = jnp.where(rows_at == 0, own * 0.5, own) if t == 0 else own
        values.append(scaled * square * field)
    power = jnp.sum(power, axis=(0, 1), keepdims=True)
    peak = jnp.max(peak, axis=(0, 1), keepdims=True)
    values.append(notes(row % share, 0, jnp.where(row < share, power, 0.0), peak))
    for pair in range(padded // 8):
        terms_ref[:, 0, pair], terms_ref[:, 1, pair] = packed(*values[2 * pair : 2 * pair + 2])
    pieces_ref[...] = terms_ref[...].reshape(count, padded, wide).astype(pieces_ref.dtype)

    start = pl.multiple_of(plane_at // 2 * 8, 8)
    mine = coupling_ref[pl.ds(start, 8), :] * step_size
    mine = jnp.concatenate([mine, mine], -1)
    turned = pltpu.roll(mine, 4, axis=0)
    row = lax.broadcasted_iota(jnp.int32, mine.shape, 0)
    lane = lax.broadcasted_iota(jnp.int32, mine.shape, 1)
    upper = row < share
    factor = jnp.where(upper == (plane_at % 2 == 0), mine, turned)
    mask = jnp.where(lane == plane_at * share + row % share, 1.0, 0.0)
    for group in range(padded // 8):
        scaled, kept = factor, mask
        if group == 0:
            scaled = jnp.where(upper & (block_at == 0), factor * 0.5, factor)
        if 2 * group + 1 == times:
            scaled, kept = jnp.where(upper, factor, 0.0), jnp.where(upper, mask, 0.0)
        factor_ref[8 * group : 8 * group + 8, :] = scaled
        mask_ref[8 * group : 8 * group + 8, :] = kept


def base_kernel(*refs):
    base_ref, extra_ref, terms_ref = refs[4:7]
    rows_ref, integrals_ref, step_re_ref, step_im_ref = refs[7:11]
    fetch(refs[:4], refs[7:11], refs[11])
    hist_at = lax.axis_index("hist")
    times, orbits, wide = rows_ref.shape
    count = extra_ref.shape[0]
    padded = base_ref.shape[0]
    low = low_half((orbits, wide))
    sign = jnp.where(low, half_step, -half_step)
    turn = jnp.where(low, -1.0, 1.0)
    shifted = [rows_ref[t] + swapped(integrals_ref[t]) * sign for t in range(times)]
    steps = jnp.concatenate([step_re_ref[...], step_im_ref[...]], 0)
    moved = jnp.dot(
        steps,
        jnp.concatenate(shifted, -1),
        precision=lax.Precision.HIGHEST,
        preferred_element_type=jnp.float32,
    )
    values = []
    for t in range(times):
        lanes = slice(t * wide, (t + 1) * wide)
        values.append(moved[:orbits, lanes] + swapped(moved[orbits:, lanes]) * turn)
    values.append(jnp.zeros((orbits, wide), jnp.float32))
    for pair in range(padded // 8):
        terms_ref[:, 0, pair], terms_ref[:, 1, pair] = packed(*values[2 * pair : 2 * pair + 2])
    base_ref[...] = terms_ref[hist_at // 2, hist_at % 2].reshape(padded, wide)
    parts = padded // count
    sub = lax.broadcasted_iota(jnp.int32, (8, wide), 0)
    row = lax.broadcasted_iota(jnp.int32, extra_ref.shape[1:], 0)
    for share in range(count):
        extra = jnp.zeros(row.shape, jnp.float32)
        for at in range(parts):
            group = terms_ref[share // 2, share % 2, at * (count // 8) + hist_at // 8]
            value = jnp.sum(jnp.where(sub == hist_at % 8, group, 0.0), axis=0, keepdims=True)
            high = value.astype(jnp.bfloat16).astype(jnp.float32)
            extra = jnp.where(row == at, high, extra)
            extra = jnp.where(row == parts + at, value - high, extra)
        extra_ref[share] = extra.astype(extra_ref.dtype)


def spread_kernel(blocks_ref, copies_ref):
    block = blocks_ref[lax.axis_index("hist")]
    for at in range(copies_ref.shape[0]):
        copies_ref[at] = block


def advance(arrived_ref, base_ref, restore, cells, total_cells):
    arrived = arrived_ref[:, : base_ref.shape[0]].astype(jnp.float32)
    total = jnp.sum(arrived, axis=0)
    row = lax.broadcasted_iota(jnp.int32, total.shape, 0)
    marked = (row == cells) | (row == cells + 1)
    power = jnp.sum(jnp.where(marked, total, 0.0), axis=0, keepdims=True)
    peak = jnp.max(jnp.where(row == cells + 2, jnp.max(arrived, axis=0), 0.0), axis=0, keepdims=True)
    integral = total / (1.0 + power / total_cells)
    if restore is not None:
        integral = integral * restore
    sign = jnp.where(low_half(total.shape), half_step, -half_step)
    return integral, base_ref[...] + swapped(integral) * sign, peak


def next_kernel(
    arrived_ref, factor_ref, mask_ref, piece_ref, base_ref, *, cells, total_cells
):
    count = arrived_ref.shape[0]
    padded, wide = base_ref.shape
    row = lax.broadcasted_iota(jnp.int32, (count, wide), 0)
    parts = padded // count
    gathered = [jnp.zeros((count, wide), jnp.float32) for _ in range(parts)]
    for h in range(count):
        extra = arrived_ref[h, padded:].astype(jnp.float32)
        for at in range(parts):
            value = extra[at : at + 1] + extra[parts + at : parts + at + 1]
            gathered[at] = jnp.where(row == h, value, gathered[at])
    base = jnp.concatenate(gathered, 0)
    row = lax.broadcasted_iota(jnp.int32, base.shape, 0)
    base_ref[...] = jnp.where(row < cells, base, 0.0)
    field = advance(arrived_ref, base_ref, None, cells, total_cells)[1]
    write_piece(piece_ref, field, factor_ref, mask_ref, 1.0, cells)


def guarded_kernel(
    arrived_ref, base_ref, factor_ref, mask_ref, piece_ref, restore_ref, *, cells, total_cells
):
    _, field, peak = advance(arrived_ref, base_ref, None, cells, total_cells)
    damping = jnp.where(peak > FAR, SMALL, 1.0)
    restore_ref[...] = jnp.broadcast_to(jnp.where(peak > FAR, LARGE, 1.0), restore_ref.shape)
    write_piece(piece_ref, field, factor_ref, mask_ref, damping, cells)


def last_kernel(arrived_ref, base_ref, restore_ref, row_ref, integral_ref, *, cells, total_cells):
    integral, field, _ = advance(arrived_ref, base_ref, restore_ref[0:1], cells, total_cells)
    times, share, _ = row_ref.shape
    for t in range(times):
        row_ref[t] = field[t * share : (t + 1) * share]
        integral_ref[t] = integral[t * share : (t + 1) * share]


def contract_kernel(pieces_ref, history_ref, *refs, times):
    *extra_refs, out_ref, field_ref, left_ref, terms_ref = refs
    count, padded, wide = pieces_ref.shape
    groups = padded // 8
    shares = count // 2
    orbits = wide // 2
    upper = lax.broadcasted_iota(jnp.int32, (groups, 8, wide), 1) < 4
    for k in range(2):
        for v in range(shares // 2):
            first = pieces_ref[4 * v + k].astype(jnp.float32).reshape(groups, 8, wide)
            second = pieces_ref[4 * v + 2 + k].astype(jnp.float32).reshape(groups, 8, wide)
            even = jnp.where(upper, first, pltpu.roll(second, 4, axis=1))
            odd = jnp.where(upper, pltpu.roll(first, 4, axis=1), second)
            field_ref[k, 0, :, 8 * v : 8 * v + 8, :] = even
            field_ref[k, 1, :, 8 * v : 8 * v + 8, :] = odd
    low = low_half((orbits, wide))
    for pair in range(times):
        blocks = []
        for s in (2 * pair, 2 * pair + 1):
            k, t = divmod(s, times)
            blocks.append(field_ref[k, t % 2, t // 2])
        lanes = slice(pair * wide, (pair + 1) * wide)
        left_ref[:orbits, lanes] = jnp.where(low, blocks[0], swapped(blocks[1])).astype(jnp.bfloat16)
        left_ref[orbits:, lanes] = jnp.where(low, swapped(blocks[0]), blocks[1]).astype(jnp.bfloat16)
    left = left_ref[...]
    depth = left.shape[1]
    sign = jnp.where(low, -1.0, 1.0)
    which = lax.broadcasted_iota(jnp.int32, (orbits, wide), 0) % 4
    marks = [field_ref[k, 1, groups - 1] for k in range(2)]
    power = jnp.sum(jnp.where(which < 2, marks[0] + marks[1], 0.0), axis=0, keepdims=True)
    peak = jnp.max(
        jnp.where(which == 2, jnp.maximum(marks[0], marks[1]), 0.0), axis=0, keepdims=True
    )
    for pair in range(groups):
        moments = [t for t in (2 * pair, 2 * pair + 1) if t < times]
        right = [history_ref[:, t].reshape(depth, wide) for t in moments]
        right = jnp.concatenate(right, -1) if len(right) > 1 else right[0]
        product = jnp.dot(left, right, preferred_element_type=jnp.float32)
        values = []
        for at in range(len(moments)):
            lanes = slice(at * wide, (at + 1) * wide)
            values.append(product[:orbits, lanes] + swapped(product[orbits:, lanes]) * sign)
        if len(moments) < 2:
            values.append(notes(which, 0, power, peak))
        terms_ref[:, 0, pair], terms_ref[:, 1, pair] = packed(*values)
    out_ref[:, :padded] = terms_ref[...].reshape(shares, padded, wide).astype(out_ref.dtype)
    for extra_ref in extra_refs:
        out_ref[:, padded:] = extra_ref[...]


def on_device(g_hist, g_last, integral_last, coupling, step_re, step_im):
    orbits = g_last.shape[0]
    row_count = g_last.shape[1]
    wide = 2 * orbits
    hist_size = lax.axis_size("hist")
    rows_size = lax.axis_size(ROWS)
    fan_out = rows_size // hist_size
    total_cells = row_count * rows_size * orbits
    share = orbits // hist_size
    cells = share * row_count
    padded = cells + share
    def exchange(blocks, axes):
        return lax.all_to_all(blocks, axes, split_axis=0, concat_axis=0, tiled=True)

    history = g_hist.transpose(0, 2, 1, 3)
    piece_shape = jax.ShapeDtypeStruct((padded, wide), jnp.bfloat16)
    local_shape = jax.ShapeDtypeStruct((padded, wide), jnp.float32)
    row_shape = jax.ShapeDtypeStruct((row_count, share, wide), jnp.float32)
    sizes = {"cells": cells, "total_cells": total_cells}
    pieces_shape = jax.ShapeDtypeStruct((hist_size, padded, wide), jnp.bfloat16)
    terms = pltpu.VMEM((hist_size // 2, 2, padded // 8, 8, wide), jnp.float32)
    by_time = [pltpu.VMEM((row_count, orbits, wide), jnp.float32)] * 2
    square = pltpu.VMEM((orbits, orbits), jnp.float32)
    spread, factor, mask = call(
        functools.partial(first_kernel, share=share),
        (pieces_shape, local_shape, local_shape),
        (OUTSIDE,) * 2,
        [terms, *by_time[:1], square, pltpu.SemaphoreType.DMA((2,))],
    )(
        far(g_last.transpose(1, 0, 2)),
        far(coupling),
    )
    integral_held, spread = lax.optimization_barrier((integral_last, spread))
    base, extra = call(
        base_kernel,
        (local_shape, jax.ShapeDtypeStruct((hist_size, 8, wide), jnp.bfloat16)),
        (OUTSIDE,) * 4,
        [terms, *by_time, square, square, pltpu.SemaphoreType.DMA((4,))],
    )(
        far(g_last.transpose(1, 0, 2)),
        far(integral_held.transpose(1, 0, 2)),
        far(step_re),
        far(step_im),
    )

    def contract(*operands):
        rows = padded + sum(value.shape[1] for value in operands[2:])
        return call(
            functools.partial(contract_kernel, times=row_count),
            jax.ShapeDtypeStruct((hist_size, rows, wide), jnp.bfloat16),
            (VECTORS,) * len(operands),
            [
                pltpu.VMEM((fan_out, 2, padded // 8, orbits, wide), jnp.float32),
                pltpu.VMEM((wide, fan_out * row_count * orbits), jnp.bfloat16),
                terms,
            ],
        )(*operands)

    copies_shape = jax.ShapeDtypeStruct((rows_size, padded, wide), jnp.bfloat16)
    copies = call(spread_kernel, copies_shape, (VECTORS,), (), pl.CostEstimate(flops=2000000000, bytes_accessed=400000, transcendentals=0))(exchange(spread, PLANE))
    copies, base, extra = lax.optimization_barrier((copies, base, extra))
    for iteration in range(ITERS):
        if iteration > 0:
            copies = jnp.broadcast_to(piece[None], copies_shape.shape)
        pieces = exchange(copies, ROWS)
        sent = contract(pieces, history, *([extra] if iteration == 0 else []))
        if iteration < ITERS - 1:
            sent = exchange(sent, PLANE)
        arrived = exchange(sent, "hist")
        if iteration == 0:
            piece, base_moved = call(
                functools.partial(next_kernel, **sizes), (piece_shape, local_shape), (VECTORS,) * 3
            )(arrived, factor, mask)
        elif iteration == 1:
            piece, restore = call(
                functools.partial(guarded_kernel, **sizes),
                (piece_shape, jax.ShapeDtypeStruct((8, wide), jnp.float32)),
                (VECTORS,) * 4,
            )(arrived, base_moved, factor, mask)
        else:
            new_row, new_integral = call(
                functools.partial(last_kernel, **sizes), (row_shape, row_shape), (VECTORS,) * 3
            )(arrived, base, restore)
    return new_row.transpose(1, 0, 2), new_integral.transpose(1, 0, 2)


def solution(mesh):
    split = Mesh(
        mesh.devices.reshape(mesh.shape["hist"], 4, 4, 2), ("hist", "rows_0", "rows_1", "rows_2")
    )
    return jax.shard_map(
        on_device,
        mesh=split,
        in_specs=(
            P("hist", None, ROWS, None),
            P(None, ROWS, None),
            P(None, ROWS, None),
            P(),
            P(),
            P(),
        ),
        out_specs=(P("hist", ROWS, None), P("hist", ROWS, None)),
        check_vma=False,
    )
```

```python
import functools

import jax
import jax.numpy as jnp
from jax import lax
from jax.experimental import pallas as pl
from jax.experimental.pallas import tpu as pltpu
from jax.sharding import Mesh
from jax.sharding import PartitionSpec as P

ITERS = 3
PLANE = ("rows_0", "rows_1")
ROWS = (*PLANE, "rows_2")
SMALL = 2.0**-90
LARGE = 2.0**90
FAR = 2.0**13
SMALL_VMEM = 16 * 2**20

step_size = 0.5
half_step = 0.25


VECTORS = pl.BlockSpec(memory_space=pltpu.VMEM)
OUTSIDE = pl.BlockSpec(memory_space=pltpu.HBM)


def call(kernel, shape, specs, scratch=(), cost=None):
    outs = (VECTORS,) * len(shape) if isinstance(shape, tuple) else VECTORS
    return pl.pallas_call(
        kernel,
        out_shape=shape,
        in_specs=specs,
        out_specs=outs,
        scratch_shapes=list(scratch),
        cost_estimate=cost,
        compiler_params=pltpu.CompilerParams(vmem_limit_bytes=SMALL_VMEM),
    )


def far(value):
    return pltpu.with_memory_space_constraint(value, pltpu.HBM)


def low_half(shape):
    return lax.broadcasted_iota(jnp.int32, shape, len(shape) - 1) < shape[-1] // 2


def swapped(value):
    return pltpu.roll(value, value.shape[-1] // 2, axis=value.ndim - 1)


def notes(row, first, power, peak):
    high = power.astype(jnp.bfloat16).astype(jnp.float32)
    parts = (high, power - high, peak)
    value = jnp.zeros(row.shape, jnp.float32)
    for at, part in enumerate(parts):
        value = jnp.where(row == first + at, part, value)
    return value


def write_piece(piece_ref, field, factor_ref, mask_ref, damping, cells):
    row = lax.broadcasted_iota(jnp.int32, field.shape, 0)
    square = field * field
    square = square + swapped(square)
    power = jnp.sum(square * mask_ref[...], axis=(0, 1), keepdims=True)
    peak = jnp.max(jnp.where(row < cells, square, 0.0), axis=(0, 1), keepdims=True)
    sigma = factor_ref[...] * (square * damping) * field
    piece_ref[...] = jnp.where(row < cells, sigma, notes(row, cells, power, peak)).astype(
        piece_ref.dtype
    )


def fetch(sources, held, sems):
    copies = [
        pltpu.make_async_copy(source, target, sems.at[at])
        for at, (source, target) in enumerate(zip(sources, held))
    ]
    for copy in copies:
        copy.start()
    for copy in copies:
        copy.wait()


def packed(even, odd):
    even, odd = (value.reshape(-1, 8, value.shape[-1]) for value in (even, odd))
    upper = lax.broadcasted_iota(jnp.int32, even.shape, 1) < 4
    return (
        jnp.where(upper, even, pltpu.roll(odd, 4, axis=1)),
        jnp.where(upper, pltpu.roll(even, 4, axis=1), odd),
    )


def first_kernel(source_ref, coupling_source_ref, pieces_ref, terms_ref, rows_ref, coupling_ref, sems):
    times, orbits, wide = rows_ref.shape
    count, padded, _ = pieces_ref.shape
    share = orbits // count
    fetch((source_ref, coupling_source_ref), (rows_ref, coupling_ref), sems)
    row = lax.broadcasted_iota(jnp.int32, (orbits, wide), 0)
    lane = lax.broadcasted_iota(jnp.int32, (orbits, wide), 1)
    own = coupling_ref[...] * step_size
    own = jnp.concatenate([own, own], -1)
    early = jnp.where(lax.axis_index(ROWS) == 0, own * 0.5, own)
    power = jnp.zeros((orbits, wide), jnp.float32)
    peak = jnp.zeros((orbits, wide), jnp.float32)
    for pair in range(padded // 8):
        values = []
        for t in range(2 * pair, min(2 * pair + 2, times)):
            field = rows_ref[t]
            square = field * field
            square = square + swapped(square)
            power = power + jnp.where(lane == row, square, 0.0)
            peak = jnp.maximum(peak, square)
            values.append((early if t == 0 else own) * square * field)
        if len(values) < 2:
            power = jnp.sum(power, axis=(0, 1), keepdims=True)
            peak = jnp.max(peak, axis=(0, 1), keepdims=True)
            values.append(notes(row % share, 0, jnp.where(row < share, power, 0.0), peak))
        terms_ref[:, 0, pair], terms_ref[:, 1, pair] = packed(*values)
    pieces_ref[...] = terms_ref[...].reshape(count, padded, wide).astype(pieces_ref.dtype)


def write_later(factor_ref, mask_ref, coupling_ref, times, share):
    plane_at = lax.axis_index(PLANE)
    block_at = lax.axis_index("hist") * lax.axis_size(ROWS[-1]) + lax.axis_index(ROWS[-1])
    start = pl.multiple_of(plane_at // 2 * 8, 8)
    mine = coupling_ref[pl.ds(start, 8), :] * step_size
    mine = jnp.concatenate([mine, mine], -1)
    turned = pltpu.roll(mine, 4, axis=0)
    row = lax.broadcasted_iota(jnp.int32, mine.shape, 0)
    lane = lax.broadcasted_iota(jnp.int32, mine.shape, 1)
    upper = row < share
    factor = jnp.where(upper == (plane_at % 2 == 0), mine, turned)
    mask = jnp.where(lane == plane_at * share + row % share, 1.0, 0.0)
    for group in range(factor_ref.shape[0] // 8):
        scaled, kept = factor, mask
        if group == 0:
            scaled = jnp.where(upper & (block_at == 0), factor * 0.5, factor)
        if 2 * group + 1 == times:
            scaled, kept = jnp.where(upper, factor, 0.0), jnp.where(upper, mask, 0.0)
        factor_ref[8 * group : 8 * group + 8, :] = scaled
        mask_ref[8 * group : 8 * group + 8, :] = kept


def base_kernel(*refs):
    base_ref, extra_ref, factor_ref, mask_ref, terms_ref = refs[5:10]
    rows_ref, integrals_ref, step_re_ref, step_im_ref, coupling_ref = held = refs[10:15]
    fetch(refs[:5], held, refs[15])
    hist_at = lax.axis_index("hist")
    times, orbits, wide = rows_ref.shape
    count = extra_ref.shape[0]
    padded = base_ref.shape[0]
    write_later(factor_ref, mask_ref, coupling_ref, times, orbits // count)
    low = low_half((orbits, wide))
    sign = jnp.where(low, half_step, -half_step)
    turn = jnp.where(low, -1.0, 1.0)
    shifted = [rows_ref[t] + swapped(integrals_ref[t]) * sign for t in range(times)]
    steps = jnp.concatenate([step_re_ref[...], step_im_ref[...]], 0)
    moved = jnp.dot(
        steps,
        jnp.concatenate(shifted, -1),
        precision=lax.Precision.HIGHEST,
        preferred_element_type=jnp.float32,
    )
    values = []
    for t in range(times):
        lanes = slice(t * wide, (t + 1) * wide)
        values.append(moved[:orbits, lanes] + swapped(moved[orbits:, lanes]) * turn)
    values.append(jnp.zeros((orbits, wide), jnp.float32))
    for pair in range(padded // 8):
        terms_ref[:, 0, pair], terms_ref[:, 1, pair] = packed(*values[2 * pair : 2 * pair + 2])
    base_ref[...] = terms_ref[hist_at // 2, hist_at % 2].reshape(padded, wide)
    parts = padded // count
    sub = lax.broadcasted_iota(jnp.int32, (8, wide), 0)
    row = lax.broadcasted_iota(jnp.int32, extra_ref.shape[1:], 0)
    for share in range(count):
        extra = jnp.zeros(row.shape, jnp.float32)
        for at in range(parts):
            group = terms_ref[share // 2, share % 2, at * (count // 8) + hist_at // 8]
            value = jnp.sum(jnp.where(sub == hist_at % 8, group, 0.0), axis=0, keepdims=True)
            high = value.astype(jnp.bfloat16).astype(jnp.float32)
            extra = jnp.where(row == at, high, extra)
            extra = jnp.where(row == parts + at, value - high, extra)
        extra_ref[share] = extra.astype(extra_ref.dtype)


def spread_kernel(blocks_ref, copies_ref):
    block = blocks_ref[lax.axis_index("hist")]
    for at in range(copies_ref.shape[0]):
        copies_ref[at] = block


def advance(arrived_ref, base_ref, restore, cells, total_cells):
    arrived = arrived_ref[:, : base_ref.shape[0]].astype(jnp.float32)
    total = jnp.sum(arrived, axis=0)
    row = lax.broadcasted_iota(jnp.int32, total.shape, 0)
    marked = (row == cells) | (row == cells + 1)
    power = jnp.sum(jnp.where(marked, total, 0.0), axis=0, keepdims=True)
    peak = jnp.max(jnp.where(row == cells + 2, jnp.max(arrived, axis=0), 0.0), axis=0, keepdims=True)
    integral = total / (1.0 + power / total_cells)
    if restore is not None:
        integral = integral * restore
    sign = jnp.where(low_half(total.shape), half_step, -half_step)
    return integral, base_ref[...] + swapped(integral) * sign, peak


def next_kernel(
    arrived_ref, factor_ref, mask_ref, piece_ref, base_ref, *, cells, total_cells
):
    count = arrived_ref.shape[0]
    padded, wide = base_ref.shape
    row = lax.broadcasted_iota(jnp.int32, (count, wide), 0)
    parts = padded // count
    gathered = [jnp.zeros((count, wide), jnp.float32) for _ in range(parts)]
    for h in range(count):
        extra = arrived_ref[h, padded:].astype(jnp.float32)
        for at in range(parts):
            value = extra[at : at + 1] + extra[parts + at : parts + at + 1]
            gathered[at] = jnp.where(row == h, value, gathered[at])
    base = jnp.concatenate(gathered, 0)
    row = lax.broadcasted_iota(jnp.int32, base.shape, 0)
    base_ref[...] = jnp.where(row < cells, base, 0.0)
    field = advance(arrived_ref, base_ref, None, cells, total_cells)[1]
    write_piece(piece_ref, field, factor_ref, mask_ref, 1.0, cells)


def guarded_kernel(
    arrived_ref, base_ref, factor_ref, mask_ref, piece_ref, restore_ref, *, cells, total_cells
):
    _, field, peak = advance(arrived_ref, base_ref, None, cells, total_cells)
    damping = jnp.where(peak > FAR, SMALL, 1.0)
    restore_ref[...] = jnp.broadcast_to(jnp.where(peak > FAR, LARGE, 1.0), restore_ref.shape)
    write_piece(piece_ref, field, factor_ref, mask_ref, damping, cells)


def last_kernel(arrived_ref, base_ref, restore_ref, row_ref, integral_ref, *, cells, total_cells):
    integral, field, _ = advance(arrived_ref, base_ref, restore_ref[0:1], cells, total_cells)
    times, share, _ = row_ref.shape
    for t in range(times):
        row_ref[t] = field[t * share : (t + 1) * share]
        integral_ref[t] = integral[t * share : (t + 1) * share]


def contract_kernel(pieces_ref, history_ref, *refs, times):
    *extra_refs, out_ref, field_ref, left_ref, terms_ref = refs
    count, padded, wide = pieces_ref.shape
    groups = padded // 8
    shares = count // 2
    orbits = wide // 2
    upper = lax.broadcasted_iota(jnp.int32, (groups, 8, wide), 1) < 4
    for k in range(2):
        for v in range(shares // 2):
            first = pieces_ref[4 * v + k].astype(jnp.float32).reshape(groups, 8, wide)
            second = pieces_ref[4 * v + 2 + k].astype(jnp.float32).reshape(groups, 8, wide)
            even = jnp.where(upper, first, pltpu.roll(second, 4, axis=1))
            odd = jnp.where(upper, pltpu.roll(first, 4, axis=1), second)
            field_ref[k, 0, :, 8 * v : 8 * v + 8, :] = even
            field_ref[k, 1, :, 8 * v : 8 * v + 8, :] = odd
    low = low_half((orbits, wide))
    for pair in range(times):
        blocks = []
        for s in (2 * pair, 2 * pair + 1):
            k, t = divmod(s, times)
            blocks.append(field_ref[k, t % 2, t // 2])
        lanes = slice(pair * wide, (pair + 1) * wide)
        left_ref[:orbits, lanes] = jnp.where(low, blocks[0], swapped(blocks[1])).astype(jnp.bfloat16)
        left_ref[orbits:, lanes] = jnp.where(low, swapped(blocks[0]), blocks[1]).astype(jnp.bfloat16)
    left = left_ref[...]
    depth = left.shape[1]
    sign = jnp.where(low, -1.0, 1.0)
    which = lax.broadcasted_iota(jnp.int32, (orbits, wide), 0) % 4
    marks = [field_ref[k, 1, groups - 1] for k in range(2)]
    power = jnp.sum(jnp.where(which < 2, marks[0] + marks[1], 0.0), axis=0, keepdims=True)
    peak = jnp.max(
        jnp.where(which == 2, jnp.maximum(marks[0], marks[1]), 0.0), axis=0, keepdims=True
    )
    for pair in range(groups):
        moments = [t for t in (2 * pair, 2 * pair + 1) if t < times]
        right = [history_ref[:, t].reshape(depth, wide) for t in moments]
        right = jnp.concatenate(right, -1) if len(right) > 1 else right[0]
        product = jnp.dot(left, right, preferred_element_type=jnp.float32)
        values = []
        for at in range(len(moments)):
            lanes = slice(at * wide, (at + 1) * wide)
            values.append(product[:orbits, lanes] + swapped(product[orbits:, lanes]) * sign)
        if len(moments) < 2:
            values.append(notes(which, 0, power, peak))
        terms_ref[:, 0, pair], terms_ref[:, 1, pair] = packed(*values)
    out_ref[:, :padded] = terms_ref[...].reshape(shares, padded, wide).astype(out_ref.dtype)
    for extra_ref in extra_refs:
        out_ref[:, padded:] = extra_ref[...]


def on_device(g_hist, g_last, integral_last, coupling, step_re, step_im):
    orbits = g_last.shape[0]
    row_count = g_last.shape[1]
    wide = 2 * orbits
    hist_size = lax.axis_size("hist")
    rows_size = lax.axis_size(ROWS)
    fan_out = rows_size // hist_size
    total_cells = row_count * rows_size * orbits
    share = orbits // hist_size
    cells = share * row_count
    padded = cells + share
    def exchange(blocks, axes):
        return lax.all_to_all(blocks, axes, split_axis=0, concat_axis=0, tiled=True)

    history = g_hist.transpose(0, 2, 1, 3)
    piece_shape = jax.ShapeDtypeStruct((padded, wide), jnp.bfloat16)
    local_shape = jax.ShapeDtypeStruct((padded, wide), jnp.float32)
    row_shape = jax.ShapeDtypeStruct((row_count, share, wide), jnp.float32)
    sizes = {"cells": cells, "total_cells": total_cells}
    pieces_shape = jax.ShapeDtypeStruct((hist_size, padded, wide), jnp.bfloat16)
    terms = pltpu.VMEM((hist_size // 2, 2, padded // 8, 8, wide), jnp.float32)
    by_time = [pltpu.VMEM((row_count, orbits, wide), jnp.float32)] * 2
    square = pltpu.VMEM((orbits, orbits), jnp.float32)
    spread = call(
        first_kernel,
        pieces_shape,
        (OUTSIDE,) * 2,
        [terms, *by_time[:1], square, pltpu.SemaphoreType.DMA((2,))],
    )(far(g_last.transpose(1, 0, 2)), far(coupling))
    integral_held, spread = lax.optimization_barrier((integral_last, spread))
    base, extra, factor, mask = call(
        base_kernel,
        (
            local_shape,
            jax.ShapeDtypeStruct((hist_size, 8, wide), jnp.bfloat16),
            local_shape,
            local_shape,
        ),
        (OUTSIDE,) * 5,
        [terms, *by_time, *[square] * 3, pltpu.SemaphoreType.DMA((5,))],
    )(
        far(g_last.transpose(1, 0, 2)),
        far(integral_held.transpose(1, 0, 2)),
        far(step_re),
        far(step_im),
        far(coupling),
    )

    def contract(*operands):
        rows = padded + sum(value.shape[1] for value in operands[2:])
        return call(
            functools.partial(contract_kernel, times=row_count),
            jax.ShapeDtypeStruct((hist_size, rows, wide), jnp.bfloat16),
            (VECTORS,) * len(operands),
            [
                pltpu.VMEM((fan_out, 2, padded // 8, orbits, wide), jnp.float32),
                pltpu.VMEM((wide, fan_out * row_count * orbits), jnp.bfloat16),
                terms,
            ],
        )(*operands)

    copies_shape = jax.ShapeDtypeStruct((rows_size, padded, wide), jnp.bfloat16)
    copies = call(spread_kernel, copies_shape, (VECTORS,), (), pl.CostEstimate(flops=2000000000, bytes_accessed=400000, transcendentals=0))(exchange(spread, PLANE))
    copies, base, extra = lax.optimization_barrier((copies, base, extra))
    for iteration in range(ITERS):
        if iteration > 0:
            copies = jnp.broadcast_to(piece[None], copies_shape.shape)
        pieces = exchange(copies, ROWS)
        sent = contract(pieces, history, *([extra] if iteration == 0 else []))
        if iteration < ITERS - 1:
            sent = exchange(sent, PLANE)
        arrived = exchange(sent, "hist")
        if iteration == 0:
            piece, base_moved = call(
                functools.partial(next_kernel, **sizes), (piece_shape, local_shape), (VECTORS,) * 3
            )(arrived, factor, mask)
        elif iteration == 1:
            piece, restore = call(
                functools.partial(guarded_kernel, **sizes),
                (piece_shape, jax.ShapeDtypeStruct((8, wide), jnp.float32)),
                (VECTORS,) * 4,
            )(arrived, base_moved, factor, mask)
        else:
            new_row, new_integral = call(
                functools.partial(last_kernel, **sizes), (row_shape, row_shape), (VECTORS,) * 3
            )(arrived, base, restore)
    return new_row.transpose(1, 0, 2), new_integral.transpose(1, 0, 2)


def solution(mesh):
    split = Mesh(
        mesh.devices.reshape(mesh.shape["hist"], 4, 4, 2), ("hist", "rows_0", "rows_1", "rows_2")
    )
    return jax.shard_map(
        on_device,
        mesh=split,
        in_specs=(
            P("hist", None, ROWS, None),
            P(None, ROWS, None),
            P(None, ROWS, None),
            P(),
            P(),
            P(),
        ),
        out_specs=(P("hist", ROWS, None), P("hist", ROWS, None)),
        check_vma=False,
    )
```
